128 devices in a mesh: rep: 4 (over y_hi, core), fsdp: 32 (over x, z, y_lo).
Axes of the slice: x: 4, y: 4 (y_hi: 2, y_lo: 2; y = y_hi * 2 + y_lo), z: 4, core: 2. Of those that a mesh axis runs over, the one named last changes fastest.
Arguments:
- tokens: bfloat16 [131072, 8192], P(('rep', 'fsdp')), may hold values from -24 to 24
- cotangent: bfloat16 [131072, 512], P(('rep', 'fsdp')), may hold values from -0.015625 to 0.015625
- old_weight: bfloat16 [8192, 512], P(('rep', 'fsdp')), may hold values from -0.0625 to 0.0625
- old_first: float32 [8192, 512], P(('rep', 'fsdp')), may hold values from -4 to 4
- old_second: float32 [8192, 512], P(('rep', 'fsdp')), may hold values from 0.05 to 2
- old_owner: int32 [128], replicated, may hold values from 0 to 127, each once
- new_owner: int32 [32], replicated, may hold values from 0 to 31, each once
Outputs:
- projected: bfloat16 [131072, 512], P(('rep', 'fsdp'))
- new_weight: bfloat16 [8192, 512], P(('rep', 'fsdp'))
- new_first: float32 [8192, 512], P(('rep', 'fsdp'))
- new_second: float32 [8192, 512], P(('rep', 'fsdp'))
The draws below stay inside these ranges and needn't reach their ends.
Inputs may be any that keep to these rules, and one draw needn't show every extreme that they name: `old_owner`: a permutation. `new_owner`: a permutation.
All inputs are finite; a program needn't handle non-finite values.
Results may differ from the reference program's by a relative error of at most 0.008.
Values may be sent and summed in bfloat16 or wider, within the bound.
A program may use at most 192 MiB of HBM per device.

```python
import math
import jax
import jax.numpy as jnp
from jax import lax

D = 8192
KV = 512
TOKENS = 131072
N_REP = 4
N_FSDP = 32
DEVICES = 128


def spiked(entries, stream_key, source, target, shards_of, factor):
    owner, partner = [(jnp.arange(entries.shape[dim]) // (entries.shape[dim] // shards_of)).reshape([-1 if axis == dim else 1 for axis in range(entries.ndim)]) for dim in (source, target)]
    chosen = jax.random.permutation(stream_key, shards_of)[partner]
    strong = (owner == chosen) | (owner == (partner + shards_of // 2) % shards_of)
    return jnp.where(strong, factor * entries, entries)


def steps_of(rng, dims, split, least, largest):
    def one(position, shards_of):
        steps = jax.random.uniform(jax.random.fold_in(jax.random.fold_in(rng, 6), position), (shards_of,), jnp.float32, least / len(split), largest / len(split))
        return jnp.repeat(jnp.exp(steps), dims[position] // shards_of).reshape((-1,) + (1,) * (len(dims) - position - 1))

    gain = one(*split[0])
    for cut in split[1:]:
        gain = gain * one(*cut)
    return gain


def bell_draw(rng, dims, deviation, most, pieces=(), kind=jnp.bfloat16):
    factor_of = steps_of(rng, dims, pieces, -0.22, 0.18) if pieces else 1.0
    values = jax.random.normal(rng, dims, jnp.float32) * deviation * factor_of
    return jnp.minimum(jnp.maximum(values, -most), most).astype(kind)


def gaussian_with(stream_key, dims, scale, limit, shards, heavy, kind=jnp.bfloat16):
    result = scale * jax.random.normal(stream_key, dims, jnp.float32)
    if shards:
        result = result * steps_of(stream_key, dims, shards, -0.22, 0.18)
    return jnp.clip(spiked(result, jax.random.fold_in(stream_key, 3), *heavy), -limit, limit).astype(kind)


def setup_inputs(seed: int = 0) -> dict:
    streams_of = jax.random.split(jax.random.key(seed), 8)
    tokens = gaussian_with(streams_of[0], (TOKENS, D), 1.0, 24.0, ((0, 128),), (0, 1, 128, 5.5))
    cotangent = bell_draw(streams_of[1], (TOKENS, KV), TOKENS ** -0.5, 0.015625, ((0, 128),))
    old_weight = bell_draw(streams_of[2], (D, KV), D ** -0.5, 0.0625, ((0, 128),))
    old_first = bell_draw(streams_of[3], (D, KV), 0.5, 4.0, ((0, 128),), jnp.float32)
    old_second = jnp.clip(jnp.exp(math.log(2.0) - 3.6888794 * jax.random.uniform(streams_of[4], (D, KV), jnp.float32) ** steps_of(streams_of[4], (D, KV), ((0, 128),), -0.2, 0.2)), 0.05, 2.0)
    old_owner = jax.random.permutation(streams_of[5], DEVICES).astype(jnp.int32)
    new_owner = jax.random.permutation(streams_of[6], N_FSDP).astype(jnp.int32)
    return dict(tokens=tokens, cotangent=cotangent, old_weight=old_weight, old_first=old_first, old_second=old_second, old_owner=old_owner, new_owner=new_owner)


beta_one = 0.9
beta_two = 0.95
learn_rate = 0.001
decay_rate = 0.1
epsilon = 1e-08
correction_one = 1.0 - 0.9 ** 10
correction_two = 1.0 - 0.95 ** 10

def reference(tokens, cotangent, old_weight, old_first, old_second, old_owner, new_owner):
    row_block = D // DEVICES
    strip = D * KV // (DEVICES * DEVICES)
    slot_ids = jnp.arange(DEVICES, dtype=jnp.int32)
    inverse = jnp.zeros((DEVICES,), jnp.int32).at[old_owner.astype(jnp.int32)].set(slot_ids)
    placing = jnp.take(new_owner.astype(jnp.int32), slot_ids % N_FSDP) * N_REP + slot_ids // N_FSDP

    def logical(source):
        held = jnp.take(source.reshape(DEVICES, DEVICES, strip), inverse, axis=0)
        return jnp.transpose(held, (1, 0, 2)).reshape(D, KV)

    def placed(source):
        return jnp.take(source.reshape(DEVICES, row_block, KV), placing, axis=0).reshape(D, KV)
    weight = logical(old_weight)
    moment_one = logical(old_first)
    moment_two = logical(old_second)
    projected = jnp.dot(tokens, weight, preferred_element_type=jnp.float32).astype(jnp.bfloat16)
    gradient = lax.dot_general(tokens, cotangent, (((0,), (0,)), ((), ())), preferred_element_type=jnp.float32)
    first_next = beta_one * moment_one + (1.0 - beta_one) * gradient
    second_next = beta_two * moment_two + (1.0 - beta_two) * gradient * gradient
    step_size = first_next / correction_one / (jnp.sqrt(second_next / correction_two) + epsilon)
    updated = (weight.astype(jnp.float32) * (1.0 - learn_rate * decay_rate) - learn_rate * step_size).astype(jnp.bfloat16)
    return (projected, placed(updated), placed(first_next), placed(second_next))
```

```python
import functools
import jax
import jax.numpy as jnp
from jax import lax
from jax.experimental import pallas as pl
from jax.experimental.pallas import tpu as pltpu
from jax.sharding import PartitionSpec as P

beta_one = 0.9
beta_two = 0.95
learn_rate = 0.001
decay_rate = 0.1
epsilon = 1e-08
correction_one = 1.0 - 0.9**10
correction_two = 1.0 - 0.95**10

MESH = pl.DeviceIdType.MESH
F32 = jnp.float32
BF16 = jnp.bfloat16
ROWS = 1024
D = 8192
KV = 512

RS_COLORS = (
    (("x", "y", "z"), (0, 48), (0, 256)),
    (("y", "z", "x"), (0, 48), (256, 256)),
    (("z", "x", "y"), (48, 16), (0, 512)),
)
AG_COLORS = (
    (("z", "y", "x"), (0, 48)),
    (("x", "z", "y"), (48, 48)),
    (("y", "x", "z"), (96, 32)),
)


def cut(spec):
    starts, sizes = [], []
    for axis in ("x", "z", "y"):
        kind, value = spec[axis]
        if axis == "y":
            if kind == "at":
                starts += [lax.rem(value, 2), value // 2]
                sizes += [1, 1]
            elif kind == "half":
                starts += [value, 0]
                sizes += [1, 2]
            else:
                starts += [0, 0]
                sizes += [2, 2]
        else:
            if kind == "at":
                starts.append(value)
                sizes.append(1)
            elif kind == "half":
                starts.append(2 * value)
                sizes.append(2)
            else:
                starts.append(0)
                sizes.append(4)
    return starts, sizes


ALL = ("all", 0)


class View:
    def __init__(self, ref, spec, rows, cols):
        self.ref, self.rows, self.cols = ref, rows, cols
        self.starts, self.sizes = cut(spec)

    @property
    def at(self):
        lead = tuple(pl.ds(s, n) for s, n in zip(self.starts, self.sizes))
        return self.ref.at[lead + (pl.ds(*self.rows), pl.ds(*self.cols))]

    def index(self, i):
        return tuple(s + k for s, k in zip(self.starts, i)) + (
            pl.ds(*self.rows),
            pl.ds(*self.cols),
        )


def own(ref, sizes, rows, cols, offset=(0, 0, 0, 0)):
    v = View.__new__(View)
    v.ref, v.rows, v.cols = ref, (0, rows), (0, cols)
    v.starts, v.sizes = list(offset), list(sizes)
    return v


def add_views(dst, sources, dtype):
    sizes = dst.sizes
    count = sizes[0] * sizes[1] * sizes[2] * sizes[3]

    def step(n, carry):
        i3 = lax.rem(n, sizes[3])
        n = n // sizes[3]
        i2 = lax.rem(n, sizes[2])
        n = n // sizes[2]
        i1 = lax.rem(n, sizes[1])
        i0 = n // sizes[1]
        i = (i0, i1, i2, i3)
        total = sources[0].ref[sources[0].index(i)].astype(F32)
        for s in sources[1:]:
            total = total + s.ref[s.index(i)].astype(F32)
        dst.ref[dst.index(i)] = total.astype(dtype)
        return carry

    lax.fori_loop(0, count, step, 0)


def kernel(
    nown_ref, place_ref, tok_hbm, cot_ref, w_ref,
    out_ref, grad_ref,
    tok, G, W, part, recv, S, perm,
    ra0, rb0, sa0, sb0, t30, t40,
    ra1, rb1, sa1, sb1, t31, t41,
    ra2, rb2, sa2, sb2, t32, t42,
    tok_sem, own_sem,
    ag_s, ag_r, die_s, die_r, ex_s, ex_r, rs_s, rs_r,
):
    r = lax.axis_index("rep")
    f = lax.axis_index("fsdp")
    yh, core = r // 2, lax.rem(r, 2)
    x, z, yl = f // 8, lax.rem(f // 2, 4), lax.rem(f, 2)
    me = {"x": x, "y": yh * 2 + yl, "z": z, "c": core}
    landing = ((ra0, rb0, sa0, sb0, t30, t40), (ra1, rb1, sa1, sb1, t31, t41), (ra2, rb2, sa2, sb2, t32, t42))

    def device(**moved):
        p = dict(me, **moved)
        return ((p["y"] // 2) * 2 + p["c"], p["x"] * 8 + p["z"] * 2 + lax.rem(p["y"], 2))

    def ring(axis, d):
        return lax.rem(me[axis] + d, 4)

    def send(src, dst, ss, rs, to):
        return pltpu.make_async_remote_copy(
            src_ref=src, dst_ref=dst, send_sem=ss, recv_sem=rs, device_id=to, device_id_type=MESH
        )

    tok_copies = [
        pltpu.make_async_copy(
            tok_hbm.at[:, pl.ds(256 * q, 256)], tok.at[q], tok_sem.at[q]
        )
        for q in range(32)
    ]
    own_copy = pltpu.make_async_copy(w_ref, G.at[x, z, yl, yh, core], own_sem)
    own_copy.start()
    for c in tok_copies:
        c.start()

    barrier = pltpu.get_barrier_semaphore()
    for axis in ("x", "y", "z"):
        for d in (1, 2, 3):
            pl.semaphore_signal(barrier, inc=1, device_id=device(**{axis: ring(axis, d)}), device_id_type=MESH)
    partner = device(c=1 - core)
    pl.semaphore_signal(barrier, inc=1, device_id=partner, device_id_type=MESH)
    rho = lax.broadcasted_iota(jnp.int32, (256, 256), 0)
    kap = lax.broadcasted_iota(jnp.int32, (256, 256), 1)
    perm[...] = (kap == lax.rem(rho, 16) * 16 + rho // 16).astype(F32).astype(BF16)
    pl.semaphore_wait(barrier, 10)
    own_copy.wait()

    def gbox(spec, blocks):
        starts, sizes = cut(spec)
        lead = tuple(pl.ds(s, n) for s, n in zip(starts, sizes))
        return G.at[lead + (pl.ds(core, 1), pl.ds(*blocks), slice(None))]

    def ag_line(k):
        axes, blocks = AG_COLORS[k]
        a = axes[0]
        box = gbox({t: ("at", me[t]) for t in axes}, blocks)
        return [
            send(box, box, ag_s.at[k, d - 1], ag_r.at[k, d - 1], device(**{a: ring(a, d)}))
            for d in (1, 2, 3)
        ]

    def ag_plane(k):
        axes, blocks = AG_COLORS[k]
        a = axes[1]
        box = gbox({axes[0]: ALL, a: ("at", me[a]), axes[2]: ("at", me[axes[2]])}, blocks)
        return [
            send(box, box, ag_s.at[k, 2 + d], ag_r.at[k, 2 + d], device(**{a: ring(a, d)}))
            for d in (1, 2, 3)
        ]

    def ag_box(k, at, half=None):
        axes, blocks = AG_COLORS[k]
        first = ALL if half is None else ("half", half)
        return gbox({axes[0]: first, axes[1]: ALL, axes[2]: ("at", at)}, blocks)

    def ag_far(k):
        a = AG_COLORS[k][0][2]
        box = ag_box(k, me[a])
        return [
            send(box, box, ag_s.at[k, 6 + i], ag_r.at[k, 6 + i], device(**{a: ring(a, d)}))
            for i, d in enumerate((1, 3))
        ]

    def ag_relay(k):
        a = AG_COLORS[k][0][2]
        up = ag_box(k, ring(a, 3), 0)
        down = ag_box(k, ring(a, 1), 1)
        return [
            send(up, up, ag_s.at[k, 8], ag_r.at[k, 8], device(**{a: ring(a, 1)})),
            send(down, down, ag_s.at[k, 9], ag_r.at[k, 9], device(**{a: ring(a, 3)})),
        ]

    def die(k, d):
        a = AG_COLORS[k][0][2]
        box = ag_box(k, ring(a, d))
        return send(box, box, die_s.at[k, d], die_r.at[k, d], partner)

    def start(copies):
        for c in copies:
            c.start()

    def arrived(copies):
        for c in copies:
            c.wait_recv()

    colors = range(3)
    line = [c for k in colors for c in ag_line(k)]
    plane = [c for k in colors for c in ag_plane(k)]
    far = [c for k in colors for c in ag_far(k)]
    relay = [c for k in colors for c in ag_relay(k)]
    dies = [[die(k, d) for k in colors] for d in range(4)]

    start(line)
    arrived(line)
    start(plane)
    for c in tok_copies:
        c.wait()

    def grad_step(n, carry):
        g = n // 8
        m = lax.rem(n, 8)
        block = lax.dot_general(
            tok[nown_ref[n]], cot_ref[...], (((0,), (0,)), ((), ())), preferred_element_type=F32
        ).astype(BF16)
        for i in range(4):
            part[g, m // 2, lax.rem(m, 2), i // 2, i % 2] = block[64 * i : 64 * i + 64]
        return carry

    def exchange(g):
        return send(
            part.at[g, :, :, :, 1 - core], recv.at[g], ex_s.at[g], ex_r.at[g], partner
        )

    def gradient(lo, hi):
        lax.fori_loop(lo, hi, grad_step, 0)

    gradient(0, 4)
    arrived(plane)
    start(far)
    start(dies[0])
    gradient(4, 8)
    exchange(0).start()
    gradient(8, 16)
    exchange(1).start()
    gradient(16, 24)
    exchange(2).start()
    arrived(far)
    start(relay)
    start(dies[1])
    start(dies[3])
    gradient(24, 32)
    exchange(3).start()

    def chip_sum(g):
        exchange(g).wait_recv()

        def step(n, carry):
            i3 = lax.rem(n, 2)
            i2 = lax.rem(n // 2, 2)
            i1 = n // 4
            S[g, i1, i2, i3] = (
                part[g, i1, i2, i3, core].astype(F32) + recv[g, i1, i2, i3].astype(F32)
            ).astype(BF16)
            return carry

        lax.fori_loop(0, 16, step, 0)

    for g in range(4):
        chip_sum(g)

    def rs(k):
        (a1, a2, a3), rows, cols = RS_COLORS[k]
        la, lb, xa, xb, l3, l4 = landing[k]
        up, down = device(**{a1: ring(a1, 1)}), device(**{a1: ring(a1, 3)})

        def sv(p1, s2, s3=ALL):
            return View(S, {a1: ("at", p1), a2: s2, a3: s3}, rows, cols)

        h0, h1 = ("half", 0), ("half", 1)
        mine, nxt, prv, opp = me[a1], ring(a1, 1), ring(a1, 3), ring(a1, 2)
        hs = sv(opp, h0).sizes
        fs = sv(opp, ALL).sizes
        hoff = [0 if p == q else p for p, q in zip(hs, fs)]
        nr, nc = rows[1], cols[1]
        la_v, lb_v = own(la, hs, nr, nc), own(lb, hs, nr, nc)
        xa0, xa1 = own(xa, hs, nr, nc), own(xa, hs, nr, nc, hoff)
        xb0, xb1 = own(xb, hs, nr, nc), own(xb, hs, nr, nc, hoff)
        first = [
            send(sv(opp, h0).at, la_v.at, rs_s.at[k, 0], rs_r.at[k, 0], up),
            send(sv(opp, h1).at, lb_v.at, rs_s.at[k, 1], rs_r.at[k, 1], down),
            send(sv(nxt, h1).at, xa1.at, rs_s.at[k, 2], rs_r.at[k, 2], up),
            send(sv(prv, h0).at, xb0.at, rs_s.at[k, 3], rs_r.at[k, 3], down),
        ]
        second = [
            send(sv(nxt, h0).at, xa0.at, rs_s.at[k, 4], rs_r.at[k, 4], up),
            send(sv(prv, h1).at, xb1.at, rs_s.at[k, 5], rs_r.at[k, 5], down),
        ]

        def fold_first():
            add_views(sv(nxt, h0), [sv(nxt, h0), la_v], BF16)
            add_views(sv(prv, h1), [sv(prv, h1), lb_v], BF16)

        full = sv(mine, ALL)

        def fold_second():
            add_views(full, [full, own(xa, fs, nr, nc), own(xb, fs, nr, nc)], BF16)

        def uv(p2):
            return sv(mine, ("at", p2))

        us = uv(0).sizes
        l3_v = [own(l3.at[d], us, nr, nc) for d in range(3)]
        third = [
            send(uv(ring(a2, d)).at, l3_v[d - 1].at, rs_s.at[k, 5 + d], rs_r.at[k, 5 + d], device(**{a2: ring(a2, d)}))
            for d in (1, 2, 3)
        ]

        def fold_third():
            add_views(uv(me[a2]), [uv(me[a2])] + l3_v, BF16)

        def vv(p3):
            return sv(mine, ("at", me[a2]), ("at", p3))

        l4_v = [own(l4.at[d], [1, 1, 1, 1], nr, nc) for d in range(3)]
        fourth = [
            send(vv(ring(a3, d)).at, l4_v[d - 1].at, rs_s.at[k, 8 + d], rs_r.at[k, 8 + d], device(**{a3: ring(a3, d)}))
            for d in (1, 2, 3)
        ]

        def fold_fourth():
            zero = (0, 0, 0, 0)
            v = vv(me[a3])
            total = v.ref[v.index(zero)].astype(F32)
            for w in l4_v:
                total = total + w.ref[w.index(zero)].astype(F32)
            grad_ref[pl.ds(*rows), pl.ds(*cols)] = total

        return first, fold_first, second, fold_second, third, fold_third, fourth, fold_fourth

    plans = [rs(k) for k in colors]
    first = [c for p in plans for c in p[0]]
    second = [c for p in plans for c in p[2]]
    third = [c for p in plans for c in p[4]]
    fourth = [c for p in plans for c in p[6]]

    start(first)

    arrived(relay)
    start(dies[2])
    for d in (0, 1, 3, 2):
        arrived(dies[d])

    def place(s, b):
        return G[
            place_ref[s, 0], place_ref[s, 1], place_ref[s, 2], place_ref[s, 3], place_ref[s, 4],
            pl.ds(pl.multiple_of(b, 16), 16), :,
        ]

    def assemble(n, carry):
        b0 = (n // 4) * 16
        j0 = lax.rem(n, 4) * 16
        halves = [
            jnp.concatenate([place(2 * (j0 + t) + h, b0) for t in range(16)], axis=0)
            for h in range(2)
        ]
        got = jnp.dot(perm[...], jnp.concatenate(halves, axis=1), preferred_element_type=F32).astype(BF16)
        for b in range(16):
            W[pl.ds(pl.multiple_of((b0 + b) * 64 + j0, 16), 16), :] = got[16 * b : 16 * b + 16]
        return carry

    lax.fori_loop(0, 32, assemble, 0)

    for c in first[0:2] + first[4:6] + first[8:10]:
        c.wait_recv()
    for p in plans:
        p[1]()
    start(second)

    def project(m, carry):
        at = pl.multiple_of(m * 256, 256)
        rows = jnp.concatenate([tok[q, pl.ds(at, 256), :] for q in range(32)], axis=1)
        out_ref[pl.ds(at, 256), :] = jnp.dot(rows, W[...], preferred_element_type=F32).astype(BF16)
        return carry

    lax.fori_loop(0, 2, project, 0)
    for c in first[2:4] + first[6:8] + first[10:12] + second:
        c.wait_recv()
    for p in plans:
        p[3]()
    start(third)
    lax.fori_loop(2, 4, project, 0)
    arrived(third)
    for p in plans:
        p[5]()
    start(fourth)
    arrived(fourth)
    for p in plans:
        p[7]()

    for c in line + plane + far + relay + [c for d in dies for c in d]:
        c.wait_send()
    for g in range(4):
        exchange(g).wait_send()
    for c in first + second + third + fourth:
        c.wait_send()


def landing_shapes():
    shapes = []
    at = ("at", 0)
    for (a1, a2, a3), rows, cols in RS_COLORS:
        n, m = rows[1], cols[1]

        def size(spec):
            return tuple(static_sizes(spec))

        half = size({a1: "at", a2: "half", a3: "all"}) + (n, m)
        full = size({a1: "at", a2: "all", a3: "all"}) + (n, m)
        line = size({a1: "at", a2: "at", a3: "all"}) + (n, m)
        shapes += [
            pltpu.VMEM(half, BF16), pltpu.VMEM(half, BF16),
            pltpu.VMEM(full, BF16), pltpu.VMEM(full, BF16),
            pltpu.VMEM((3,) + line, BF16), pltpu.VMEM((3, 1, 1, 1, 1, n, m), BF16),
        ]
    return shapes


def static_sizes(spec):
    sizes = []
    for axis in ("x", "z", "y"):
        kind = spec[axis]
        if axis == "y":
            sizes += {"at": [1, 1], "half": [1, 2], "all": [2, 2]}[kind]
        else:
            sizes += {"at": [1], "half": [2], "all": [4]}[kind]
    return sizes


def fused(new_owner, places, tokens, cotangent, shard):
    smem = pl.BlockSpec(memory_space=pltpu.SMEM)
    vmem = pl.BlockSpec(memory_space=pltpu.VMEM)
    dma = pltpu.SemaphoreType.DMA
    return pl.pallas_call(
        kernel,
        out_shape=(
            jax.ShapeDtypeStruct((ROWS, KV), BF16),
            jax.ShapeDtypeStruct((64, KV), F32),
        ),
        in_specs=[smem, smem, pl.BlockSpec(memory_space=pl.ANY), vmem, vmem],
        out_specs=(vmem, vmem),
        scratch_shapes=[
            pltpu.VMEM((32, ROWS, 256), BF16),
            pltpu.VMEM((4, 4, 2, 2, 2, 128, 256), BF16),
            pltpu.VMEM((D, KV), BF16),
            pltpu.VMEM((4, 4, 2, 2, 2, 64, KV), BF16),
            pltpu.VMEM((4, 4, 2, 2, 64, KV), BF16),
            pltpu.VMEM((4, 4, 2, 2, 64, KV), BF16),
            pltpu.VMEM((256, 256), BF16),
        ]
        + landing_shapes()
        + [
            dma((32,)), dma,
            dma((3, 10)), dma((3, 10)), dma((3, 4)), dma((3, 4)),
            dma((4,)), dma((4,)), dma((3, 12)), dma((3, 12)),
        ],
        compiler_params=pltpu.CompilerParams(
            collective_id=0, has_side_effects=True, vmem_limit_bytes=67_000_000
        ),
        name="gather_grad_project",
    )(new_owner, places, tokens, cotangent, shard)


def body(tokens, cotangent, old_weight, old_first, old_second, old_owner, new_owner):
    devices, shards, groups, strip = 128, 32, 4, 256
    slot_ids = jnp.arange(devices, dtype=jnp.int32)
    inverse = jnp.sum(
        jnp.where(old_owner[None, :] == slot_ids[:, None], slot_ids[None, :], 0), axis=1
    ).astype(jnp.int32)
    r, f = inverse // shards, inverse % shards
    places = jnp.stack([f // 8, (f // 2) % 4, f % 2, r // 2, r % 2], axis=1)
    placing = (new_owner[None, :] * groups + jnp.arange(groups, dtype=jnp.int32)[:, None]).reshape(devices)

    shard = old_weight.reshape(devices, strip)
    stacked = jnp.concatenate(
        [old_first.reshape(devices, strip).astype(BF16), old_second.reshape(devices, strip).astype(BF16), shard],
        axis=1,
    )
    outgoing = jnp.take(stacked, placing, axis=0)
    arrived = lax.all_to_all(outgoing, ("rep", "fsdp"), split_axis=0, concat_axis=0, tiled=True)
    projected, gradient = fused(new_owner, places, tokens, cotangent, shard)
    moved = jnp.take(arrived, inverse, axis=0).astype(F32)
    first_rows = moved[:, :strip].reshape(64, KV)
    second_rows = moved[:, strip : 2 * strip].reshape(64, KV)
    weight_rows = moved[:, 2 * strip :].reshape(64, KV)

    first_next = beta_one * first_rows + (1.0 - beta_one) * gradient
    second_next = beta_two * second_rows + (1.0 - beta_two) * gradient * gradient
    step_size = first_next / correction_one / (jnp.sqrt(second_next / correction_two) + epsilon)
    updated = (weight_rows * (1.0 - learn_rate * decay_rate) - learn_rate * step_size).astype(BF16)
    return (projected, updated, first_next, second_next)


def solution(mesh):
    rows = P(("rep", "fsdp"), None)
    return jax.shard_map(
        body,
        mesh=mesh,
        in_specs=(rows, rows, rows, rows, rows, P(), P()),
        out_specs=(rows, rows, rows, rows),
        check_vma=False,
    )
```

```python
import functools
import jax
import jax.numpy as jnp
from jax import lax
from jax.experimental import pallas as pl
from jax.experimental.pallas import tpu as pltpu
from jax.sharding import PartitionSpec as P

beta_one = 0.9
beta_two = 0.95
learn_rate = 0.001
decay_rate = 0.1
epsilon = 1e-08
correction_one = 1.0 - 0.9**10
correction_two = 1.0 - 0.95**10

MESH = pl.DeviceIdType.MESH
F32 = jnp.float32
BF16 = jnp.bfloat16
ROWS = 1024
D = 8192
KV = 512

RS_COLORS = (
    (("x", "y", "z"), (0, 48), (0, 256)),
    (("y", "z", "x"), (0, 48), (256, 256)),
    (("z", "x", "y"), (48, 16), (0, 512)),
)
AG_COLORS = (
    (("z", "y", "x"), (0, 48)),
    (("x", "z", "y"), (48, 48)),
    (("y", "x", "z"), (96, 32)),
)


def cut(spec):
    starts, sizes = [], []
    for axis in ("x", "z", "y"):
        kind, value = spec[axis]
        if axis == "y":
            if kind == "at":
                starts += [lax.rem(value, 2), value // 2]
                sizes += [1, 1]
            elif kind == "half":
                starts += [value, 0]
                sizes += [1, 2]
            else:
                starts += [0, 0]
                sizes += [2, 2]
        else:
            if kind == "at":
                starts.append(value)
                sizes.append(1)
            elif kind == "half":
                starts.append(2 * value)
                sizes.append(2)
            else:
                starts.append(0)
                sizes.append(4)
    return starts, sizes


ALL = ("all", 0)


class View:
    def __init__(self, ref, spec, rows, cols):
        self.ref, self.rows, self.cols = ref, rows, cols
        self.starts, self.sizes = cut(spec)

    @property
    def at(self):
        lead = tuple(pl.ds(s, n) for s, n in zip(self.starts, self.sizes))
        return self.ref.at[lead + (pl.ds(*self.rows), pl.ds(*self.cols))]

    def index(self, i):
        return tuple(s + k for s, k in zip(self.starts, i)) + (
            pl.ds(*self.rows),
            pl.ds(*self.cols),
        )


def own(ref, sizes, rows, cols, offset=(0, 0, 0, 0)):
    v = View.__new__(View)
    v.ref, v.rows, v.cols = ref, (0, rows), (0, cols)
    v.starts, v.sizes = list(offset), list(sizes)
    return v


def add_views(dst, sources, dtype):
    sizes = dst.sizes
    count = sizes[0] * sizes[1] * sizes[2] * sizes[3]

    def step(n, carry):
        i3 = lax.rem(n, sizes[3])
        n = n // sizes[3]
        i2 = lax.rem(n, sizes[2])
        n = n // sizes[2]
        i1 = lax.rem(n, sizes[1])
        i0 = n // sizes[1]
        i = (i0, i1, i2, i3)
        total = sources[0].ref[sources[0].index(i)].astype(F32)
        for s in sources[1:]:
            total = total + s.ref[s.index(i)].astype(F32)
        dst.ref[dst.index(i)] = total.astype(dtype)
        return carry

    lax.fori_loop(0, count, step, 0)


def iota(shape, dim):
    return lax.broadcasted_iota(jnp.int32, shape, dim)


def one_hot(mask):
    return mask.astype(F32).astype(BF16)


def stack_halves(v):
    return jnp.concatenate([v[:, :256], v[:, 256:]], axis=0)


def kernel(
    nown_ref, inv_ref, nown_vec, owner_vec, tok_hbm, cot_ref, w_ref, first_ref, second_ref,
    out_ref, grad_ref, m_ref, wrow_ref,
    tok, G, W, part, recv, S,
    M0, C1, Y1, XZ, X1, Z1,
    *rest,
):
    (tok_sem, ag_s, ag_r, die_s, die_r, ex_s, ex_r, rs_s, rs_r, mv_s, mv_r) = rest[-11:]
    landing = (rest[0:6], rest[6:12], rest[12:18])
    r = lax.axis_index("rep")
    f = lax.axis_index("fsdp")
    yh, core = r // 2, lax.rem(r, 2)
    x, z, yl = f // 8, lax.rem(f // 2, 4), lax.rem(f, 2)
    me = {"x": x, "y": yh * 2 + yl, "z": z, "c": core}

    def device(**moved):
        p = dict(me, **moved)
        return ((p["y"] // 2) * 2 + p["c"], p["x"] * 8 + p["z"] * 2 + lax.rem(p["y"], 2))

    def ring(axis, d):
        return lax.rem(me[axis] + d, 4)

    def send(src, dst, ss, rs, to):
        return pltpu.make_async_remote_copy(
            src_ref=src, dst_ref=dst, send_sem=ss, recv_sem=rs, device_id=to, device_id_type=MESH
        )

    def start(copies):
        for c in copies:
            c.start()

    def arrived(copies):
        for c in copies:
            c.wait_recv()

    everything = []

    def keep(copies):
        everything.extend(copies)
        return copies

    barrier = pltpu.get_barrier_semaphore()
    for axis in ("x", "y", "z"):
        for d in (1, 2, 3):
            pl.semaphore_signal(barrier, inc=1, device_id=device(**{axis: ring(axis, d)}), device_id_type=MESH)
    partner = device(c=1 - core)
    pl.semaphore_signal(barrier, inc=1, device_id=partner, device_id_type=MESH)

    tok_copies = [
        pltpu.make_async_copy(tok_hbm.at[:, pl.ds(256 * q, 256)], tok.at[q], tok_sem.at[q])
        for q in range(32)
    ]
    start(tok_copies)

    sq = (128, 128)
    split = one_hot(iota(sq, 1) == lax.rem(iota(sq, 0), 2) * 64 + iota(sq, 0) // 2)
    G[x, z, yl, yh, core] = jnp.dot(split, stack_halves(w_ref[...]), preferred_element_type=F32).astype(BF16)

    d = iota(sq, 1)
    dc, dyl, dyh, dx, dz = d // 64, lax.rem(d // 32, 2), lax.rem(d // 16, 2), lax.rem(d // 4, 4), lax.rem(d, 4)
    pick = one_hot((iota(sq, 0) == dx * 8 + dz * 2 + dyl)[:32])
    block = 4.0 * jnp.dot(nown_vec[...].astype(F32).astype(BF16), pick, preferred_element_type=F32)
    block = block + (dyh * 2 + dc)[:1].astype(F32)
    sp = iota(sq, 0)
    choose = one_hot(block == (2 * lax.rem(sp, 64) + sp // 64).astype(F32))
    moments = jnp.concatenate(
        [stack_halves(first_ref[...].astype(BF16)), stack_halves(second_ref[...].astype(BF16))], axis=1
    )
    moved = lax.dot_general(choose, moments, (((0,), (0,)), ((), ())), preferred_element_type=F32).astype(BF16)
    for i in range(8):
        M0[i // 4, (i // 2) % 2, i % 2] = moved[16 * i : 16 * i + 16]

    def gbox(spec, blocks):
        starts, sizes = cut(spec)
        lead = tuple(pl.ds(s, n) for s, n in zip(starts, sizes))
        return G.at[lead + (pl.ds(core, 1), pl.ds(*blocks), slice(None))]

    def ag_line(k):
        axes, blocks = AG_COLORS[k]
        a = axes[0]
        box = gbox({t: ("at", me[t]) for t in axes}, blocks)
        return [
            send(box, box, ag_s.at[k, d - 1], ag_r.at[k, d - 1], device(**{a: ring(a, d)}))
            for d in (1, 2, 3)
        ]

    def ag_plane(k):
        axes, blocks = AG_COLORS[k]
        a = axes[1]
        box = gbox({axes[0]: ALL, a: ("at", me[a]), axes[2]: ("at", me[axes[2]])}, blocks)
        return [
            send(box, box, ag_s.at[k, 2 + d], ag_r.at[k, 2 + d], device(**{a: ring(a, d)}))
            for d in (1, 2, 3)
        ]

    def ag_box(k, at, half=None):
        axes, blocks = AG_COLORS[k]
        first = ALL if half is None else ("half", half)
        return gbox({axes[0]: first, axes[1]: ALL, axes[2]: ("at", at)}, blocks)

    def ag_far(k):
        a = AG_COLORS[k][0][2]
        box = ag_box(k, me[a])
        return [
            send(box, box, ag_s.at[k, 6 + i], ag_r.at[k, 6 + i], device(**{a: ring(a, d)}))
            for i, d in enumerate((1, 3))
        ]

    def ag_relay(k):
        a = AG_COLORS[k][0][2]
        up = ag_box(k, ring(a, 3), 0)
        down = ag_box(k, ring(a, 1), 1)
        return [
            send(up, up, ag_s.at[k, 8], ag_r.at[k, 8], device(**{a: ring(a, 1)})),
            send(down, down, ag_s.at[k, 9], ag_r.at[k, 9], device(**{a: ring(a, 3)})),
        ]

    def die(k, d):
        a = AG_COLORS[k][0][2]
        box = ag_box(k, ring(a, d))
        return send(box, box, die_s.at[k, d], die_r.at[k, d], partner)

    colors = range(3)
    line = keep([c for k in colors for c in ag_line(k)])
    plane = keep([c for k in colors for c in ag_plane(k)])
    far = keep([c for k in colors for c in ag_far(k)])
    relay = keep([c for k in colors for c in ag_relay(k)])
    dies = [keep([die(k, d) for k in colors]) for d in range(4)]

    pl.semaphore_wait(barrier, 10)
    start(line)

    mv_c = keep([send(M0.at[1 - core], C1.at[core], mv_s.at[0], mv_r.at[0], partner)])
    start(mv_c)
    C1[core] = M0[core]
    mv_y = keep([
        send(
            C1.at[:, lax.rem(ring("y", d), 2), ring("y", d) // 2], Y1.at[yl, yh],
            mv_s.at[d], mv_r.at[d], device(y=ring("y", d)),
        )
        for d in (1, 2, 3)
    ])
    mv_x = keep([
        send(XZ.at[ring("x", d)], X1.at[x], mv_s.at[3 + d], mv_r.at[3 + d], device(x=ring("x", d)))
        for d in (1, 2, 3)
    ])
    mv_z = keep([
        send(X1.at[:, ring("z", d)], Z1.at[:, z], mv_s.at[6 + d], mv_r.at[6 + d], device(z=ring("z", d)))
        for d in (1, 2, 3)
    ])

    arrived(line)
    start(plane)
    arrived(mv_c)
    start(mv_y)
    Y1[yl, yh] = C1[:, yl, yh]
    for c in tok_copies:
        c.wait()

    def grad_step(n, carry):
        g = n // 8
        m = lax.rem(n, 8)
        block = lax.dot_general(
            tok[nown_ref[n]], cot_ref[...], (((0,), (0,)), ((), ())), preferred_element_type=F32
        ).astype(BF16)
        for i in range(4):
            part[g, m // 2, lax.rem(m, 2), i // 2, i % 2] = block[64 * i : 64 * i + 64]
        return carry

    exchange = keep([
        send(part.at[g, :, :, :, 1 - core], recv.at[g], ex_s.at[g], ex_r.at[g], partner)
        for g in range(4)
    ])

    def gradient(lo, hi):
        lax.fori_loop(lo, hi, grad_step, 0, unroll=4)

    gradient(0, 8)
    exchange[0].start()
    arrived(plane)
    start(far)
    start(dies[0])
    arrived(mv_y)
    rows = Y1[...].reshape(128, 512)
    swap = one_hot(iota(sq, 1) == lax.rem(iota(sq, 0), 8) * 16 + iota(sq, 0) // 8)
    XZ[...] = jnp.dot(swap, rows, preferred_element_type=F32).astype(BF16).reshape(4, 4, 8, 512)
    start(mv_x)
    X1[x] = XZ[x]
    gradient(8, 16)
    exchange[1].start()
    gradient(16, 24)
    exchange[2].start()
    arrived(mv_x)
    start(mv_z)
    Z1[:, z] = X1[:, z]
    gradient(24, 32)
    exchange[3].start()
    arrived(far)
    start(relay)
    start(dies[1])
    start(dies[3])

    def chip_sum(g):
        exchange[g].wait_recv()

        def step(n, carry):
            i3 = lax.rem(n, 2)
            i2 = lax.rem(n // 2, 2)
            i1 = n // 4
            S[g, i1, i2, i3] = (
                part[g, i1, i2, i3, core].astype(F32) + recv[g, i1, i2, i3].astype(F32)
            ).astype(BF16)
            return carry

        lax.fori_loop(0, 16, step, 0)

    for g in range(4):
        chip_sum(g)

    def rs(k):
        (a1, a2, a3), rows, cols = RS_COLORS[k]
        la, lb, xa, xb, l3, l4 = landing[k]
        up, down = device(**{a1: ring(a1, 1)}), device(**{a1: ring(a1, 3)})

        def sv(p1, s2, s3=ALL):
            return View(S, {a1: ("at", p1), a2: s2, a3: s3}, rows, cols)

        h0, h1 = ("half", 0), ("half", 1)
        mine, nxt, prv, opp = me[a1], ring(a1, 1), ring(a1, 3), ring(a1, 2)
        hs = sv(opp, h0).sizes
        fs = sv(opp, ALL).sizes
        hoff = [0 if p == q else p for p, q in zip(hs, fs)]
        nr, nc = rows[1], cols[1]
        la_v, lb_v = own(la, hs, nr, nc), own(lb, hs, nr, nc)
        xa0, xa1 = own(xa, hs, nr, nc), own(xa, hs, nr, nc, hoff)
        xb0, xb1 = own(xb, hs, nr, nc), own(xb, hs, nr, nc, hoff)
        first = [
            send(sv(opp, h0).at, la_v.at, rs_s.at[k, 0], rs_r.at[k, 0], up),
            send(sv(opp, h1).at, lb_v.at, rs_s.at[k, 1], rs_r.at[k, 1], down),
            send(sv(nxt, h1).at, xa1.at, rs_s.at[k, 2], rs_r.at[k, 2], up),
            send(sv(prv, h0).at, xb0.at, rs_s.at[k, 3], rs_r.at[k, 3], down),
        ]
        second = [
            send(sv(nxt, h0).at, xa0.at, rs_s.at[k, 4], rs_r.at[k, 4], up),
            send(sv(prv, h1).at, xb1.at, rs_s.at[k, 5], rs_r.at[k, 5], down),
        ]

        def fold_first():
            add_views(sv(nxt, h0), [sv(nxt, h0), la_v], BF16)
            add_views(sv(prv, h1), [sv(prv, h1), lb_v], BF16)

        full = sv(mine, ALL)

        def fold_second():
            add_views(full, [full, own(xa, fs, nr, nc), own(xb, fs, nr, nc)], BF16)

        def uv(p2):
            return sv(mine, ("at", p2))

        us = uv(0).sizes
        l3_v = [own(l3.at[d], us, nr, nc) for d in range(3)]
        third = [
            send(uv(ring(a2, d)).at, l3_v[d - 1].at, rs_s.at[k, 5 + d], rs_r.at[k, 5 + d], device(**{a2: ring(a2, d)}))
            for d in (1, 2, 3)
        ]

        def fold_third():
            add_views(uv(me[a2]), [uv(me[a2])] + l3_v, BF16)

        def vv(p3):
            return sv(mine, ("at", me[a2]), ("at", p3))

        l4_v = [own(l4.at[d], [1, 1, 1, 1], nr, nc) for d in range(3)]
        fourth = [
            send(vv(ring(a3, d)).at, l4_v[d - 1].at, rs_s.at[k, 8 + d], rs_r.at[k, 8 + d], device(**{a3: ring(a3, d)}))
            for d in (1, 2, 3)
        ]

        def fold_fourth():
            zero = (0, 0, 0, 0)
            v = vv(me[a3])
            total = v.ref[v.index(zero)].astype(F32)
            for w in l4_v:
                total = total + w.ref[w.index(zero)].astype(F32)
            grad_ref[pl.ds(*rows), pl.ds(*cols)] = total

        return first, fold_first, second, fold_second, third, fold_third, fourth, fold_fourth

    plans = [rs(k) for k in colors]
    first = keep([c for p in plans for c in p[0]])
    second = keep([c for p in plans for c in p[2]])
    third = keep([c for p in plans for c in p[4]])
    fourth = keep([c for p in plans for c in p[6]])

    start(first)

    arrived(relay)
    start(dies[2])

    def place(s, b):
        i = inv_ref[s]
        return G[
            i // 32, lax.rem(i // 8, 4), lax.rem(i // 4, 2), lax.rem(i // 2, 2), lax.rem(i, 2),
            pl.ds(pl.multiple_of(b, 16), 16), :,
        ]

    def assemble(n, carry):
        b0 = (n // 4) * 16
        j0 = lax.rem(n, 4) * 16
        for h in range(2):
            got = jnp.swapaxes(jnp.stack([place(2 * (j0 + t) + h, b0) for t in range(16)], axis=0), 0, 1)
            for b in range(16):
                W[b0 + b, pl.ds(pl.multiple_of(j0, 16), 16), pl.ds(256 * h, 256)] = got[b]
        return carry

    def project(m):
        at = 256 * m
        rows = jnp.concatenate([tok[q, pl.ds(at, 256), :] for q in range(32)], axis=1)
        out_ref[pl.ds(at, 256), :] = jnp.dot(
            rows, W[...].reshape(D, KV), preferred_element_type=F32
        ).astype(BF16)

    for d in (0, 1, 3, 2):
        arrived(dies[d])
    lax.fori_loop(0, 32, assemble, 0)
    for p in plans:
        arrived(p[0][:2])
        p[1]()
        start(p[2])
    project(0)
    project(1)
    for p in plans:
        arrived(p[0][2:] + p[2])
        p[3]()
        start(p[4])
    project(2)
    project(3)
    for p in plans:
        arrived(p[4])
        p[5]()
        start(p[6])

    arrived(mv_z)
    owner = jnp.dot(
        owner_vec[...].astype(F32).astype(BF16),
        one_hot(iota(sq, 0) == lax.rem(iota(sq, 1), 4) * 32 + iota(sq, 1) // 4),
        preferred_element_type=F32,
    )
    strips = Z1[...].reshape(128, 512)
    halves = [
        jnp.dot(
            one_hot(owner == (2 * iota((64, 128), 0) + h).astype(F32)), strips, preferred_element_type=F32
        ).astype(BF16)
        for h in range(2)
    ]
    for i in range(2):
        for h in range(2):
            m_ref[i, :, pl.ds(256 * h, 256)] = halves[h][:, 256 * i : 256 * i + 256]
    wrow_ref[...] = W[nown_ref[f] * 4 + r]
    for p in plans:
        arrived(p[6])
        p[7]()
    for c in everything:
        c.wait_send()


def landing_shapes():
    shapes = []
    at = ("at", 0)
    for (a1, a2, a3), rows, cols in RS_COLORS:
        n, m = rows[1], cols[1]

        def size(spec):
            return tuple(static_sizes(spec))

        half = size({a1: "at", a2: "half", a3: "all"}) + (n, m)
        full = size({a1: "at", a2: "all", a3: "all"}) + (n, m)
        line = size({a1: "at", a2: "at", a3: "all"}) + (n, m)
        shapes += [
            pltpu.VMEM(half, BF16), pltpu.VMEM(half, BF16),
            pltpu.VMEM(full, BF16), pltpu.VMEM(full, BF16),
            pltpu.VMEM((3,) + line, BF16), pltpu.VMEM((3, 1, 1, 1, 1, n, m), BF16),
        ]
    return shapes


def static_sizes(spec):
    sizes = []
    for axis in ("x", "z", "y"):
        kind = spec[axis]
        if axis == "y":
            sizes += {"at": [1, 1], "half": [1, 2], "all": [2, 2]}[kind]
        else:
            sizes += {"at": [1], "half": [2], "all": [4]}[kind]
    return sizes


def fused(new_owner, inverse, old_owner, tokens, cotangent, old_weight, old_first, old_second):
    smem = pl.BlockSpec(memory_space=pltpu.SMEM)
    vmem = pl.BlockSpec(memory_space=pltpu.VMEM)
    dma = pltpu.SemaphoreType.DMA
    return pl.pallas_call(
        kernel,
        out_shape=(
            jax.ShapeDtypeStruct((ROWS, KV), BF16),
            jax.ShapeDtypeStruct((64, KV), F32),
            jax.ShapeDtypeStruct((2, 64, KV), BF16),
            jax.ShapeDtypeStruct((64, KV), BF16),
        ),
        in_specs=[smem, smem, vmem, vmem, pl.BlockSpec(memory_space=pl.ANY)] + [vmem] * 4,
        out_specs=(vmem,) * 4,
        scratch_shapes=[
            pltpu.VMEM((32, ROWS, 256), BF16),
            pltpu.VMEM((4, 4, 2, 2, 2, 128, 256), BF16),
            pltpu.VMEM((128, 64, KV), BF16),
            pltpu.VMEM((4, 4, 2, 2, 2, 64, KV), BF16),
            pltpu.VMEM((4, 4, 2, 2, 64, KV), BF16),
            pltpu.VMEM((4, 4, 2, 2, 64, KV), BF16),
            pltpu.VMEM((2, 2, 2, 16, 512), BF16),
            pltpu.VMEM((2, 2, 2, 16, 512), BF16),
            pltpu.VMEM((2, 2, 2, 16, 512), BF16),
            pltpu.VMEM((4, 4, 8, 512), BF16),
            pltpu.VMEM((4, 4, 8, 512), BF16),
            pltpu.VMEM((4, 4, 8, 512), BF16),
        ]
        + landing_shapes()
        + [
            dma((32,)),
            dma((3, 10)), dma((3, 10)), dma((3, 4)), dma((3, 4)),
            dma((4,)), dma((4,)), dma((3, 12)), dma((3, 12)),
            dma((10,)), dma((10,)),
        ],
        compiler_params=pltpu.CompilerParams(
            collective_id=0, has_side_effects=True, vmem_limit_bytes=67_000_000
        ),
        name="gather_grad_project",
    )(
        new_owner, inverse, new_owner.reshape(1, 32), old_owner.reshape(1, 128),
        tokens, cotangent, old_weight, old_first, old_second,
    )


def body(tokens, cotangent, old_weight, old_first, old_second, old_owner, new_owner):
    slot_ids = jnp.arange(128, dtype=jnp.int32)
    at = (slot_ids % 32) * 4 + slot_ids // 32
    inverse = jnp.sum(
        jnp.where(old_owner[None, :] == slot_ids[:, None], at[None, :], 0), axis=1
    ).astype(jnp.int32)
    projected, gradient, moments, weight_rows = fused(
        new_owner, inverse, old_owner, tokens, cotangent, old_weight, old_first, old_second
    )
    first_next = beta_one * moments[0].astype(F32) + (1.0 - beta_one) * gradient
    second_next = beta_two * moments[1].astype(F32) + (1.0 - beta_two) * gradient * gradient
    step_size = first_next / correction_one / (jnp.sqrt(second_next / correction_two) + epsilon)
    updated = (weight_rows.astype(F32) * (1.0 - learn_rate * decay_rate) - learn_rate * step_size).astype(BF16)
    return (projected, updated, first_next, second_next)


def solution(mesh):
    rows = P(("rep", "fsdp"), None)
    return jax.shard_map(
        body,
        mesh=mesh,
        in_specs=(rows, rows, rows, rows, rows, P(), P()),
        out_specs=(rows, rows, rows, rows),
        check_vma=False,
    )
```

```python
import functools
import jax
import jax.numpy as jnp
from jax import lax
from jax.experimental import pallas as pl
from jax.experimental.pallas import tpu as pltpu
from jax.sharding import PartitionSpec as P

beta_one = 0.9
beta_two = 0.95
learn_rate = 0.001
decay_rate = 0.1
epsilon = 1e-08
correction_one = 1.0 - 0.9**10
correction_two = 1.0 - 0.95**10

MESH = pl.DeviceIdType.MESH
F32 = jnp.float32
BF16 = jnp.bfloat16
ROWS = 1024
D = 8192
KV = 512

RS_COLORS = (
    (("x", "y", "z"), (0, 48), (0, 256)),
    (("y", "z", "x"), (0, 48), (256, 256)),
    (("z", "x", "y"), (48, 16), (0, 512)),
)
AG_COLORS = (
    (("z", "y", "x"), (0, 48)),
    (("x", "z", "y"), (48, 48)),
    (("y", "x", "z"), (96, 32)),
)


def cut(spec):
    starts, sizes = [], []
    for axis in ("x", "z", "y"):
        kind, value = spec[axis]
        if axis == "y":
            if kind == "at":
                starts += [lax.rem(value, 2), value // 2]
                sizes += [1, 1]
            elif kind == "half":
                starts += [value, 0]
                sizes += [1, 2]
            else:
                starts += [0, 0]
                sizes += [2, 2]
        else:
            if kind == "at":
                starts.append(value)
                sizes.append(1)
            elif kind == "half":
                starts.append(2 * value)
                sizes.append(2)
            else:
                starts.append(0)
                sizes.append(4)
    return starts, sizes


ALL = ("all", 0)


class View:
    def __init__(self, ref, spec, rows, cols):
        self.ref, self.rows, self.cols = ref, rows, cols
        self.starts, self.sizes = cut(spec)

    @property
    def at(self):
        lead = tuple(pl.ds(s, n) for s, n in zip(self.starts, self.sizes))
        return self.ref.at[lead + (pl.ds(*self.rows), pl.ds(*self.cols))]

    def index(self, i):
        return tuple(s + k for s, k in zip(self.starts, i)) + (
            pl.ds(*self.rows),
            pl.ds(*self.cols),
        )


def own(ref, sizes, rows, cols, offset=(0, 0, 0, 0)):
    v = View.__new__(View)
    v.ref, v.rows, v.cols = ref, (0, rows), (0, cols)
    v.starts, v.sizes = list(offset), list(sizes)
    return v


def add_views(dst, sources, dtype):
    sizes = dst.sizes
    count = sizes[0] * sizes[1] * sizes[2] * sizes[3]

    def step(n, carry):
        i3 = lax.rem(n, sizes[3])
        n = lax.div(n, sizes[3])
        i2 = lax.rem(n, sizes[2])
        n = lax.div(n, sizes[2])
        i1 = lax.rem(n, sizes[1])
        i0 = lax.div(n, sizes[1])
        i = (i0, i1, i2, i3)
        total = sources[0].ref[sources[0].index(i)].astype(F32)
        for s in sources[1:]:
            total = total + s.ref[s.index(i)].astype(F32)
        dst.ref[dst.index(i)] = total.astype(dtype)
        return carry

    lax.fori_loop(0, count, step, 0)


def iota(shape, dim):
    return lax.broadcasted_iota(jnp.int32, shape, dim)


def one_hot(mask):
    return mask.astype(F32).astype(BF16)


def stack_halves(v):
    return jnp.concatenate([v[:, :256], v[:, 256:]], axis=0)


def kernel(
    nown_ref, inv_ref, nown_vec, owner_vec, tok_hbm, cot_ref, w_ref, first_ref, second_ref,
    out_ref, grad_ref, m_ref, wrow_ref,
    tok, G, W, part, recv, S,
    M0, C1, Y1, XZ, X1, Z1,
    *rest,
):
    (tok_sem, ag_s, ag_r, die_s, die_r, ex_s, ex_r, rs_s, rs_r, mv_s, mv_r) = rest[-11:]
    landing = (rest[0:6], rest[6:12], rest[12:18])
    r = lax.axis_index("rep")
    f = lax.axis_index("fsdp")
    yh, core = r // 2, lax.rem(r, 2)
    x, z, yl = f // 8, lax.rem(f // 2, 4), lax.rem(f, 2)
    me = {"x": x, "y": yh * 2 + yl, "z": z, "c": core}

    def device(**moved):
        p = dict(me, **moved)
        return ((p["y"] // 2) * 2 + p["c"], p["x"] * 8 + p["z"] * 2 + lax.rem(p["y"], 2))

    def ring(axis, d):
        return lax.rem(me[axis] + d, 4)

    def send(src, dst, ss, rs, to):
        return pltpu.make_async_remote_copy(
            src_ref=src, dst_ref=dst, send_sem=ss, recv_sem=rs, device_id=to, device_id_type=MESH
        )

    def start(copies):
        for c in copies:
            c.start()

    def arrived(copies):
        for c in copies:
            c.wait_recv()

    everything = []

    def keep(copies):
        everything.extend(copies)
        return copies

    barrier = pltpu.get_barrier_semaphore()
    for axis in ("x", "y", "z"):
        for d in (1, 2, 3):
            pl.semaphore_signal(barrier, inc=1, device_id=device(**{axis: ring(axis, d)}), device_id_type=MESH)
    partner = device(c=1 - core)
    pl.semaphore_signal(barrier, inc=1, device_id=partner, device_id_type=MESH)

    tok_copies = [
        pltpu.make_async_copy(tok_hbm.at[:, pl.ds(256 * q, 256)], tok.at[q], tok_sem.at[q])
        for q in range(32)
    ]
    start(tok_copies)

    sq = (128, 128)
    split = one_hot(iota(sq, 1) == lax.rem(iota(sq, 0), 2) * 64 + iota(sq, 0) // 2)
    G[x, z, yl, yh, core] = jnp.dot(split, stack_halves(w_ref[...]), preferred_element_type=F32).astype(BF16)

    def gbox(spec, blocks):
        starts, sizes = cut(spec)
        lead = tuple(pl.ds(s, n) for s, n in zip(starts, sizes))
        return G.at[lead + (pl.ds(core, 1), pl.ds(*blocks), slice(None))]

    def ag_line(k):
        axes, blocks = AG_COLORS[k]
        a = axes[0]
        box = gbox({t: ("at", me[t]) for t in axes}, blocks)
        return [
            send(box, box, ag_s.at[k, d - 1], ag_r.at[k, d - 1], device(**{a: ring(a, d)}))
            for d in (1, 2, 3)
        ]

    def ag_plane(k):
        axes, blocks = AG_COLORS[k]
        a = axes[1]
        box = gbox({axes[0]: ALL, a: ("at", me[a]), axes[2]: ("at", me[axes[2]])}, blocks)
        return [
            send(box, box, ag_s.at[k, 2 + d], ag_r.at[k, 2 + d], device(**{a: ring(a, d)}))
            for d in (1, 2, 3)
        ]

    def ag_box(k, at, half=None):
        axes, blocks = AG_COLORS[k]
        first = ALL if half is None else ("half", half)
        return gbox({axes[0]: first, axes[1]: ALL, axes[2]: ("at", at)}, blocks)

    def ag_far(k):
        a = AG_COLORS[k][0][2]
        box = ag_box(k, me[a])
        return [
            send(box, box, ag_s.at[k, 6 + i], ag_r.at[k, 6 + i], device(**{a: ring(a, d)}))
            for i, d in enumerate((1, 3))
        ]

    def ag_relay(k):
        a = AG_COLORS[k][0][2]
        up = ag_box(k, ring(a, 3), 0)
        down = ag_box(k, ring(a, 1), 1)
        return [
            send(up, up, ag_s.at[k, 8], ag_r.at[k, 8], device(**{a: ring(a, 1)})),
            send(down, down, ag_s.at[k, 9], ag_r.at[k, 9], device(**{a: ring(a, 3)})),
        ]

    def die(k, d):
        a = AG_COLORS[k][0][2]
        box = ag_box(k, ring(a, d))
        return send(box, box, die_s.at[k, d], die_r.at[k, d], partner)

    colors = range(3)
    line = keep([c for k in colors for c in ag_line(k)])
    plane = keep([c for k in colors for c in ag_plane(k)])
    far = keep([c for k in colors for c in ag_far(k)])
    relay = keep([c for k in colors for c in ag_relay(k)])
    dies = [keep([die(k, d) for k in colors]) for d in range(4)]

    pl.semaphore_wait(barrier, 10)
    start(line)

    d = iota(sq, 1)
    dc, dyl, dyh, dx, dz = d // 64, lax.rem(d // 32, 2), lax.rem(d // 16, 2), lax.rem(d // 4, 4), lax.rem(d, 4)
    pick = one_hot((iota(sq, 0) == dx * 8 + dz * 2 + dyl)[:32])
    block = 4.0 * jnp.dot(nown_vec[...].astype(F32).astype(BF16), pick, preferred_element_type=F32)
    block = block + (dyh * 2 + dc)[:1].astype(F32)
    sp = iota(sq, 0)
    choose = one_hot(block == (2 * lax.rem(sp, 64) + sp // 64).astype(F32))
    moments = jnp.concatenate(
        [stack_halves(first_ref[...].astype(BF16)), stack_halves(second_ref[...].astype(BF16))], axis=1
    )
    moved = lax.dot_general(choose, moments, (((0,), (0,)), ((), ())), preferred_element_type=F32).astype(BF16)
    for i in range(8):
        M0[i // 4, (i // 2) % 2, i % 2] = moved[16 * i : 16 * i + 16]

    mv_c = keep([send(M0.at[1 - core], C1.at[core], mv_s.at[0], mv_r.at[0], partner)])
    start(mv_c)
    C1[core] = M0[core]
    mv_y = keep([
        send(
            C1.at[:, lax.rem(ring("y", d), 2), ring("y", d) // 2], Y1.at[yl, yh],
            mv_s.at[d], mv_r.at[d], device(y=ring("y", d)),
        )
        for d in (1, 2, 3)
    ])
    mv_x = keep([
        send(XZ.at[ring("x", d)], X1.at[x], mv_s.at[3 + d], mv_r.at[3 + d], device(x=ring("x", d)))
        for d in (1, 2, 3)
    ])
    mv_z = keep([
        send(X1.at[:, ring("z", d)], Z1.at[:, z], mv_s.at[6 + d], mv_r.at[6 + d], device(z=ring("z", d)))
        for d in (1, 2, 3)
    ])

    arrived(line)
    start(plane)
    for c in tok_copies:
        c.wait()

    def grad_step(n, carry):
        g = lax.div(n, 8)
        m = lax.rem(n, 8)
        block = lax.dot_general(
            tok[nown_ref[n]], cot_ref[...], (((0,), (0,)), ((), ())), preferred_element_type=F32
        ).astype(BF16)
        for i in range(4):
            part[g, lax.div(m, 2), lax.rem(m, 2), i // 2, i % 2] = block[64 * i : 64 * i + 64]
        return carry

    exchange = keep([
        send(part.at[g, :, :, :, 1 - core], recv.at[g], ex_s.at[g], ex_r.at[g], partner)
        for g in range(4)
    ])

    def gradient(lo, hi):
        lax.fori_loop(lo, hi, grad_step, 0, unroll=8)

    gradient(0, 8)
    exchange[0].start()
    arrived(mv_c)
    start(mv_y)
    Y1[yl, yh] = C1[:, yl, yh]
    gradient(8, 16)
    exchange[1].start()
    arrived(plane)
    start(far)
    start(dies[0])
    gradient(16, 24)
    exchange[2].start()
    arrived(mv_y)
    rows = Y1[...].reshape(128, 512)
    swap = one_hot(iota(sq, 1) == lax.rem(iota(sq, 0), 8) * 16 + iota(sq, 0) // 8)
    XZ[...] = jnp.dot(swap, rows, preferred_element_type=F32).astype(BF16).reshape(4, 4, 8, 512)
    start(mv_x)
    X1[x] = XZ[x]
    gradient(24, 32)
    exchange[3].start()

    def chip_sum(g):
        exchange[g].wait_recv()

        def step(n, carry):
            i3 = lax.rem(n, 2)
            i2 = lax.rem(lax.div(n, 2), 2)
            i1 = lax.div(n, 4)
            S[g, i1, i2, i3] = (
                part[g, i1, i2, i3, core].astype(F32) + recv[g, i1, i2, i3].astype(F32)
            ).astype(BF16)
            return carry

        lax.fori_loop(0, 16, step, 0)

    for g in range(4):
        chip_sum(g)

    def rs(k):
        (a1, a2, a3), rows, cols = RS_COLORS[k]
        la, lb, xa, xb, l3, l4 = landing[k]
        up, down = device(**{a1: ring(a1, 1)}), device(**{a1: ring(a1, 3)})

        def sv(p1, s2, s3=ALL):
            return View(S, {a1: ("at", p1), a2: s2, a3: s3}, rows, cols)

        h0, h1 = ("half", 0), ("half", 1)
        mine, nxt, prv, opp = me[a1], ring(a1, 1), ring(a1, 3), ring(a1, 2)
        hs = sv(opp, h0).sizes
        fs = sv(opp, ALL).sizes
        hoff = [0 if p == q else p for p, q in zip(hs, fs)]
        nr, nc = rows[1], cols[1]
        la_v, lb_v = own(la, hs, nr, nc), own(lb, hs, nr, nc)
        xa0, xa1 = own(xa, hs, nr, nc), own(xa, hs, nr, nc, hoff)
        xb0, xb1 = own(xb, hs, nr, nc), own(xb, hs, nr, nc, hoff)
        first = [
            send(sv(opp, h0).at, la_v.at, rs_s.at[k, 0], rs_r.at[k, 0], up),
            send(sv(opp, h1).at, lb_v.at, rs_s.at[k, 1], rs_r.at[k, 1], down),
            send(sv(nxt, h1).at, xa1.at, rs_s.at[k, 2], rs_r.at[k, 2], up),
            send(sv(prv, h0).at, xb0.at, rs_s.at[k, 3], rs_r.at[k, 3], down),
        ]
        second = [
            send(sv(nxt, h0).at, xa0.at, rs_s.at[k, 4], rs_r.at[k, 4], up),
            send(sv(prv, h1).at, xb1.at, rs_s.at[k, 5], rs_r.at[k, 5], down),
        ]

        def fold_first():
            add_views(sv(nxt, h0), [sv(nxt, h0), la_v], BF16)
            add_views(sv(prv, h1), [sv(prv, h1), lb_v], BF16)

        full = sv(mine, ALL)

        def fold_second():
            add_views(full, [full, own(xa, fs, nr, nc), own(xb, fs, nr, nc)], BF16)

        def uv(p2):
            return sv(mine, ("at", p2))

        us = uv(0).sizes
        l3_v = [own(l3.at[d], us, nr, nc) for d in range(3)]
        third = [
            send(uv(ring(a2, d)).at, l3_v[d - 1].at, rs_s.at[k, 5 + d], rs_r.at[k, 5 + d], device(**{a2: ring(a2, d)}))
            for d in (1, 2, 3)
        ]

        def fold_third():
            add_views(uv(me[a2]), [uv(me[a2])] + l3_v, BF16)

        def vv(p3):
            return sv(mine, ("at", me[a2]), ("at", p3))

        l4_v = [own(l4.at[d], [1, 1, 1, 1], nr, nc) for d in range(3)]
        fourth = [
            send(vv(ring(a3, d)).at, l4_v[d - 1].at, rs_s.at[k, 8 + d], rs_r.at[k, 8 + d], device(**{a3: ring(a3, d)}))
            for d in (1, 2, 3)
        ]

        def fold_fourth():
            zero = (0, 0, 0, 0)
            v = vv(me[a3])
            total = v.ref[v.index(zero)].astype(F32)
            for w in l4_v:
                total = total + w.ref[w.index(zero)].astype(F32)
            grad_ref[pl.ds(*rows), pl.ds(*cols)] = total

        return first, fold_first, second, fold_second, third, fold_third, fourth, fold_fourth

    plans = [rs(k) for k in colors]
    first = keep([c for p in plans for c in p[0]])
    second = keep([c for p in plans for c in p[2]])
    third = keep([c for p in plans for c in p[4]])
    fourth = keep([c for p in plans for c in p[6]])

    start(first)
    arrived(far)
    start(relay)
    start(dies[1])
    start(dies[3])
    arrived(mv_x)
    start(mv_z)
    Z1[:, z] = X1[:, z]

    arrived(relay)
    start(dies[2])

    def slot(s):
        i = inv_ref[s]
        return (
            lax.div(i, 32), lax.rem(lax.div(i, 8), 4), lax.rem(lax.div(i, 4), 2), lax.rem(lax.div(i, 2), 2), lax.rem(i, 2),
        )

    def assemble(n, carry):
        j0 = pl.multiple_of(n * 16, 16)
        for h in range(2):
            slots = [slot(2 * (n * 16 + t) + h) for t in range(16)]
            for b0 in range(0, 128, 16):
                got = jnp.swapaxes(jnp.stack([G[i + (pl.ds(b0, 16), slice(None))] for i in slots], axis=0), 0, 1)
                for b in range(16):
                    W[b0 + b, pl.ds(j0, 16), pl.ds(256 * h, 256)] = got[b]
        return carry

    def project(m):
        at = 256 * m
        rows = jnp.concatenate([tok[q, pl.ds(at, 256), :] for q in range(32)], axis=1)
        out_ref[pl.ds(at, 256), :] = jnp.dot(
            rows, W[...].reshape(D, KV), preferred_element_type=F32
        ).astype(BF16)

    for d in (0, 1, 3, 2):
        arrived(dies[d])
    lax.fori_loop(0, 4, assemble, 0)
    for p in plans:
        arrived(p[0][:2])
        p[1]()
        start(p[2])
    project(0)
    project(1)
    for p in plans:
        arrived(p[0][2:] + p[2])
        p[3]()
        start(p[4])
    project(2)
    project(3)
    for p in plans:
        arrived(p[4])
        p[5]()
        start(p[6])

    arrived(mv_z)
    owner = jnp.dot(
        owner_vec[...].astype(F32).astype(BF16),
        one_hot(iota(sq, 0) == lax.rem(iota(sq, 1), 4) * 32 + iota(sq, 1) // 4),
        preferred_element_type=F32,
    )
    strips = Z1[...].reshape(128, 512)
    halves = [
        jnp.dot(
            one_hot(owner == (2 * iota((64, 128), 0) + h).astype(F32)), strips, preferred_element_type=F32
        ).astype(BF16)
        for h in range(2)
    ]
    for i in range(2):
        for h in range(2):
            m_ref[i, :, pl.ds(256 * h, 256)] = halves[h][:, 256 * i : 256 * i + 256]
    wrow_ref[...] = W[nown_ref[f] * 4 + r]
    for p in plans:
        arrived(p[6])
        p[7]()
    for c in everything:
        c.wait_send()


def landing_shapes():
    shapes = []
    at = ("at", 0)
    for (a1, a2, a3), rows, cols in RS_COLORS:
        n, m = rows[1], cols[1]

        def size(spec):
            return tuple(static_sizes(spec))

        half = size({a1: "at", a2: "half", a3: "all"}) + (n, m)
        full = size({a1: "at", a2: "all", a3: "all"}) + (n, m)
        line = size({a1: "at", a2: "at", a3: "all"}) + (n, m)
        shapes += [
            pltpu.VMEM(half, BF16), pltpu.VMEM(half, BF16),
            pltpu.VMEM(full, BF16), pltpu.VMEM(full, BF16),
            pltpu.VMEM((3,) + line, BF16), pltpu.VMEM((3, 1, 1, 1, 1, n, m), BF16),
        ]
    return shapes


def static_sizes(spec):
    sizes = []
    for axis in ("x", "z", "y"):
        kind = spec[axis]
        if axis == "y":
            sizes += {"at": [1, 1], "half": [1, 2], "all": [2, 2]}[kind]
        else:
            sizes += {"at": [1], "half": [2], "all": [4]}[kind]
    return sizes


def fused(new_owner, inverse, old_owner, tokens, cotangent, old_weight, old_first, old_second):
    smem = pl.BlockSpec(memory_space=pltpu.SMEM)
    vmem = pl.BlockSpec(memory_space=pltpu.VMEM)
    dma = pltpu.SemaphoreType.DMA
    return pl.pallas_call(
        kernel,
        out_shape=(
            jax.ShapeDtypeStruct((ROWS, KV), BF16),
            jax.ShapeDtypeStruct((64, KV), F32),
            jax.ShapeDtypeStruct((2, 64, KV), BF16),
            jax.ShapeDtypeStruct((64, KV), BF16),
        ),
        in_specs=[smem, smem, vmem, vmem, pl.BlockSpec(memory_space=pl.ANY)] + [vmem] * 4,
        out_specs=(vmem,) * 4,
        scratch_shapes=[
            pltpu.VMEM((32, ROWS, 256), BF16),
            pltpu.VMEM((4, 4, 2, 2, 2, 128, 256), BF16),
            pltpu.VMEM((128, 64, KV), BF16),
            pltpu.VMEM((4, 4, 2, 2, 2, 64, KV), BF16),
            pltpu.VMEM((4, 4, 2, 2, 64, KV), BF16),
            pltpu.VMEM((4, 4, 2, 2, 64, KV), BF16),
            pltpu.VMEM((2, 2, 2, 16, 512), BF16),
            pltpu.VMEM((2, 2, 2, 16, 512), BF16),
            pltpu.VMEM((2, 2, 2, 16, 512), BF16),
            pltpu.VMEM((4, 4, 8, 512), BF16),
            pltpu.VMEM((4, 4, 8, 512), BF16),
            pltpu.VMEM((4, 4, 8, 512), BF16),
        ]
        + landing_shapes()
        + [
            dma((32,)),
            dma((3, 10)), dma((3, 10)), dma((3, 4)), dma((3, 4)),
            dma((4,)), dma((4,)), dma((3, 12)), dma((3, 12)),
            dma((10,)), dma((10,)),
        ],
        compiler_params=pltpu.CompilerParams(
            collective_id=0, has_side_effects=True, vmem_limit_bytes=67_000_000
        ),
        name="gather_grad_project",
    )(
        new_owner, inverse, new_owner.reshape(1, 32), old_owner.reshape(1, 128),
        tokens, cotangent, old_weight, old_first, old_second,
    )


def body(tokens, cotangent, old_weight, old_first, old_second, old_owner, new_owner):
    slot_ids = jnp.arange(128, dtype=jnp.int32)
    at = (slot_ids % 32) * 4 + slot_ids // 32
    inverse = jnp.sum(
        jnp.where(old_owner[None, :] == slot_ids[:, None], at[None, :], 0), axis=1
    ).astype(jnp.int32)
    projected, gradient, moments, weight_rows = fused(
        new_owner, inverse, old_owner, tokens, cotangent, old_weight, old_first, old_second
    )
    first_next = beta_one * moments[0].astype(F32) + (1.0 - beta_one) * gradient
    second_next = beta_two * moments[1].astype(F32) + (1.0 - beta_two) * gradient * gradient
    step_size = first_next / correction_one / (jnp.sqrt(second_next / correction_two) + epsilon)
    updated = (weight_rows.astype(F32) * (1.0 - learn_rate * decay_rate) - learn_rate * step_size).astype(BF16)
    return (projected, updated, first_next, second_next)


def solution(mesh):
    rows = P(("rep", "fsdp"), None)
    return jax.shard_map(
        body,
        mesh=mesh,
        in_specs=(rows, rows, rows, rows, rows, P(), P()),
        out_specs=(rows, rows, rows, rows),
        check_vma=False,
    )
```

```python
import functools
import jax
import jax.numpy as jnp
from jax import lax
from jax.experimental import pallas as pl
from jax.experimental.pallas import tpu as pltpu
from jax.sharding import PartitionSpec as P

beta_one = 0.9
beta_two = 0.95
learn_rate = 0.001
decay_rate = 0.1
epsilon = 1e-08
correction_one = 1.0 - 0.9**10
correction_two = 1.0 - 0.95**10

MESH = pl.DeviceIdType.MESH
F32 = jnp.float32
BF16 = jnp.bfloat16
ROWS = 1024
D = 8192
KV = 512

RS_COLORS = (
    (("x", "y", "z"), (0, 48), (0, 256)),
    (("y", "z", "x"), (0, 48), (256, 256)),
    (("z", "x", "y"), (48, 16), (0, 512)),
)
AG_COLORS = (
    (("z", "y", "x"), (0, 48)),
    (("x", "z", "y"), (48, 48)),
    (("y", "x", "z"), (96, 32)),
)


def cut(spec):
    starts, sizes = [], []
    for axis in ("x", "z", "y"):
        kind, value = spec[axis]
        if axis == "y":
            if kind == "at":
                starts += [lax.rem(value, 2), value // 2]
                sizes += [1, 1]
            elif kind == "half":
                starts += [value, 0]
                sizes += [1, 2]
            else:
                starts += [0, 0]
                sizes += [2, 2]
        else:
            if kind == "at":
                starts.append(value)
                sizes.append(1)
            elif kind == "half":
                starts.append(2 * value)
                sizes.append(2)
            else:
                starts.append(0)
                sizes.append(4)
    return starts, sizes


ALL = ("all", 0)


class View:
    def __init__(self, ref, spec, rows, cols):
        self.ref, self.rows, self.cols = ref, rows, cols
        self.starts, self.sizes = cut(spec)

    @property
    def at(self):
        lead = tuple(pl.ds(s, n) for s, n in zip(self.starts, self.sizes))
        return self.ref.at[lead + (pl.ds(*self.rows), pl.ds(*self.cols))]

    def index(self, i):
        return tuple(s + k for s, k in zip(self.starts, i)) + (
            pl.ds(*self.rows),
            pl.ds(*self.cols),
        )


def own(ref, sizes, rows, cols, offset=(0, 0, 0, 0)):
    v = View.__new__(View)
    v.ref, v.rows, v.cols = ref, (0, rows), (0, cols)
    v.starts, v.sizes = list(offset), list(sizes)
    return v


def add_views(dst, sources, dtype):
    sizes = dst.sizes
    count = sizes[0] * sizes[1] * sizes[2] * sizes[3]

    def step(n, carry):
        i3 = lax.rem(n, sizes[3])
        n = lax.div(n, sizes[3])
        i2 = lax.rem(n, sizes[2])
        n = lax.div(n, sizes[2])
        i1 = lax.rem(n, sizes[1])
        i0 = lax.div(n, sizes[1])
        i = (i0, i1, i2, i3)
        total = sources[0].ref[sources[0].index(i)].astype(F32)
        for s in sources[1:]:
            total = total + s.ref[s.index(i)].astype(F32)
        dst.ref[dst.index(i)] = total.astype(dtype)
        return carry

    lax.fori_loop(0, count, step, 0)


def iota(shape, dim):
    return lax.broadcasted_iota(jnp.int32, shape, dim)


def one_hot(mask):
    return mask.astype(F32).astype(BF16)


def stack_halves(v):
    return jnp.concatenate([v[:, :256], v[:, 256:]], axis=0)


def kernel(
    nown_ref, inv_ref, nown_vec, owner_vec, tok_hbm, cot_hbm, first_hbm, second_hbm, w_ref,
    out_hbm, grad_ref, m_ref, wrow_ref,
    cot_ref, first_ref, second_ref, out_v, in_sem, out_sem,
    tok, G, W, part, recv, S,
    M0, C1, Y1, XZ, X1, Z1,
    *rest,
):
    (tok_sem, ag_s, ag_r, die_s, die_r, ex_s, ex_r, rs_s, rs_r, mv_s, mv_r) = rest[-11:]
    landing = (rest[0:6], rest[6:12], rest[12:18])
    r = lax.axis_index("rep")
    f = lax.axis_index("fsdp")
    yh, core = r // 2, lax.rem(r, 2)
    x, z, yl = f // 8, lax.rem(f // 2, 4), lax.rem(f, 2)
    me = {"x": x, "y": yh * 2 + yl, "z": z, "c": core}

    def device(**moved):
        p = dict(me, **moved)
        return ((p["y"] // 2) * 2 + p["c"], p["x"] * 8 + p["z"] * 2 + lax.rem(p["y"], 2))

    def ring(axis, d):
        return lax.rem(me[axis] + d, 4)

    def send(src, dst, ss, rs, to):
        return pltpu.make_async_remote_copy(
            src_ref=src, dst_ref=dst, send_sem=ss, recv_sem=rs, device_id=to, device_id_type=MESH
        )

    def start(copies):
        for c in copies:
            c.start()

    def arrived(copies):
        for c in copies:
            c.wait_recv()

    everything = []

    def keep(copies):
        everything.extend(copies)
        return copies

    barrier = pltpu.get_barrier_semaphore()
    for axis in ("x", "y", "z"):
        for d in (1, 2, 3):
            pl.semaphore_signal(barrier, inc=1, device_id=device(**{axis: ring(axis, d)}), device_id_type=MESH)
    partner = device(c=1 - core)
    pl.semaphore_signal(barrier, inc=1, device_id=partner, device_id_type=MESH)

    tok_copies = [
        pltpu.make_async_copy(tok_hbm.at[:, pl.ds(256 * q, 256)], tok.at[q], tok_sem.at[q])
        for q in range(32)
    ]
    in_copies = [
        pltpu.make_async_copy(a, b, in_sem.at[i])
        for i, (a, b) in enumerate(((first_hbm, first_ref), (second_hbm, second_ref), (cot_hbm, cot_ref)))
    ]
    start(in_copies)
    start(tok_copies)

    sq = (128, 128)
    split = one_hot(iota(sq, 1) == lax.rem(iota(sq, 0), 2) * 64 + iota(sq, 0) // 2)
    G[x, z, yl, yh, core] = jnp.dot(split, stack_halves(w_ref[...]), preferred_element_type=F32).astype(BF16)

    def gbox(spec, blocks):
        starts, sizes = cut(spec)
        lead = tuple(pl.ds(s, n) for s, n in zip(starts, sizes))
        return G.at[lead + (pl.ds(core, 1), pl.ds(*blocks), slice(None))]

    def ag_line(k):
        axes, blocks = AG_COLORS[k]
        a = axes[0]
        box = gbox({t: ("at", me[t]) for t in axes}, blocks)
        return [
            send(box, box, ag_s.at[k, d - 1], ag_r.at[k, d - 1], device(**{a: ring(a, d)}))
            for d in (1, 2, 3)
        ]

    def ag_plane(k):
        axes, blocks = AG_COLORS[k]
        a = axes[1]
        box = gbox({axes[0]: ALL, a: ("at", me[a]), axes[2]: ("at", me[axes[2]])}, blocks)
        return [
            send(box, box, ag_s.at[k, 2 + d], ag_r.at[k, 2 + d], device(**{a: ring(a, d)}))
            for d in (1, 2, 3)
        ]

    def ag_box(k, at, half=None):
        axes, blocks = AG_COLORS[k]
        first = ALL if half is None else ("half", half)
        return gbox({axes[0]: first, axes[1]: ALL, axes[2]: ("at", at)}, blocks)

    def ag_far(k):
        a = AG_COLORS[k][0][2]
        box = ag_box(k, me[a])
        return [
            send(box, box, ag_s.at[k, 6 + i], ag_r.at[k, 6 + i], device(**{a: ring(a, d)}))
            for i, d in enumerate((1, 3))
        ]

    def ag_relay(k):
        a = AG_COLORS[k][0][2]
        up = ag_box(k, ring(a, 3), 0)
        down = ag_box(k, ring(a, 1), 1)
        return [
            send(up, up, ag_s.at[k, 8], ag_r.at[k, 8], device(**{a: ring(a, 1)})),
            send(down, down, ag_s.at[k, 9], ag_r.at[k, 9], device(**{a: ring(a, 3)})),
        ]

    def die(k, d):
        a = AG_COLORS[k][0][2]
        box = ag_box(k, ring(a, d))
        return send(box, box, die_s.at[k, d], die_r.at[k, d], partner)

    colors = range(3)
    line = keep([c for k in colors for c in ag_line(k)])
    plane = keep([c for k in colors for c in ag_plane(k)])
    far = keep([c for k in colors for c in ag_far(k)])
    relay = keep([c for k in colors for c in ag_relay(k)])
    dies = [keep([die(k, d) for k in colors]) for d in range(4)]

    pl.semaphore_wait(barrier, 10)
    start(line)

    d = iota(sq, 1)
    dc, dyl, dyh, dx, dz = d // 64, lax.rem(d // 32, 2), lax.rem(d // 16, 2), lax.rem(d // 4, 4), lax.rem(d, 4)
    pick = one_hot((iota(sq, 0) == dx * 8 + dz * 2 + dyl)[:32])
    block = 4.0 * jnp.dot(nown_vec[...].astype(F32).astype(BF16), pick, preferred_element_type=F32)
    block = block + (dyh * 2 + dc)[:1].astype(F32)
    sp = iota(sq, 0)
    choose = one_hot(block == (2 * lax.rem(sp, 64) + sp // 64).astype(F32))
    in_copies[0].wait()
    in_copies[1].wait()
    moments = jnp.concatenate(
        [stack_halves(first_ref[...].astype(BF16)), stack_halves(second_ref[...].astype(BF16))], axis=1
    )
    moved = lax.dot_general(choose, moments, (((0,), (0,)), ((), ())), preferred_element_type=F32).astype(BF16)
    for i in range(8):
        M0[i // 4, (i // 2) % 2, i % 2] = moved[16 * i : 16 * i + 16]

    mv_c = keep([send(M0.at[1 - core], C1.at[core], mv_s.at[0], mv_r.at[0], partner)])
    start(mv_c)
    C1[core] = M0[core]
    mv_y = keep([
        send(
            C1.at[:, lax.rem(ring("y", d), 2), ring("y", d) // 2], Y1.at[yl, yh],
            mv_s.at[d], mv_r.at[d], device(y=ring("y", d)),
        )
        for d in (1, 2, 3)
    ])
    mv_x = keep([
        send(XZ.at[ring("x", d)], X1.at[x], mv_s.at[3 + d], mv_r.at[3 + d], device(x=ring("x", d)))
        for d in (1, 2, 3)
    ])
    mv_z = keep([
        send(X1.at[:, ring("z", d)], Z1.at[:, z], mv_s.at[6 + d], mv_r.at[6 + d], device(z=ring("z", d)))
        for d in (1, 2, 3)
    ])

    arrived(line)
    start(plane)
    in_copies[2].wait()
    for c in tok_copies:
        c.wait()

    def grad_step(n, carry):
        g = lax.div(n, 8)
        m = lax.rem(n, 8)
        block = lax.dot_general(
            tok[nown_ref[n]], cot_ref[...], (((0,), (0,)), ((), ())), preferred_element_type=F32
        ).astype(BF16)
        for i in range(4):
            part[g, lax.div(m, 2), lax.rem(m, 2), i // 2, i % 2] = block[64 * i : 64 * i + 64]
        return carry

    exchange = keep([
        send(part.at[g, :, :, :, 1 - core], recv.at[g], ex_s.at[g], ex_r.at[g], partner)
        for g in range(4)
    ])

    def gradient(lo, hi):
        lax.fori_loop(lo, hi, grad_step, 0, unroll=8)

    gradient(0, 8)
    exchange[0].start()
    arrived(mv_c)
    start(mv_y)
    Y1[yl, yh] = C1[:, yl, yh]
    gradient(8, 16)
    exchange[1].start()
    arrived(plane)
    start(far)
    start(dies[0])
    gradient(16, 24)
    exchange[2].start()
    arrived(mv_y)
    rows = Y1[...].reshape(128, 512)
    swap = one_hot(iota(sq, 1) == lax.rem(iota(sq, 0), 8) * 16 + iota(sq, 0) // 8)
    XZ[...] = jnp.dot(swap, rows, preferred_element_type=F32).astype(BF16).reshape(4, 4, 8, 512)
    start(mv_x)
    X1[x] = XZ[x]
    gradient(24, 32)
    exchange[3].start()

    def chip_sum(g):
        exchange[g].wait_recv()

        def step(n, carry):
            i3 = lax.rem(n, 2)
            i2 = lax.rem(lax.div(n, 2), 2)
            i1 = lax.div(n, 4)
            S[g, i1, i2, i3] = (
                part[g, i1, i2, i3, core].astype(F32) + recv[g, i1, i2, i3].astype(F32)
            ).astype(BF16)
            return carry

        lax.fori_loop(0, 16, step, 0)

    for g in range(4):
        chip_sum(g)

    def rs(k):
        (a1, a2, a3), rows, cols = RS_COLORS[k]
        la, lb, xa, xb, l3, l4 = landing[k]
        up, down = device(**{a1: ring(a1, 1)}), device(**{a1: ring(a1, 3)})

        def sv(p1, s2, s3=ALL):
            return View(S, {a1: ("at", p1), a2: s2, a3: s3}, rows, cols)

        h0, h1 = ("half", 0), ("half", 1)
        mine, nxt, prv, opp = me[a1], ring(a1, 1), ring(a1, 3), ring(a1, 2)
        hs = sv(opp, h0).sizes
        fs = sv(opp, ALL).sizes
        hoff = [0 if p == q else p for p, q in zip(hs, fs)]
        nr, nc = rows[1], cols[1]
        la_v, lb_v = own(la, hs, nr, nc), own(lb, hs, nr, nc)
        xa0, xa1 = own(xa, hs, nr, nc), own(xa, hs, nr, nc, hoff)
        xb0, xb1 = own(xb, hs, nr, nc), own(xb, hs, nr, nc, hoff)
        first = [
            send(sv(opp, h0).at, la_v.at, rs_s.at[k, 0], rs_r.at[k, 0], up),
            send(sv(opp, h1).at, lb_v.at, rs_s.at[k, 1], rs_r.at[k, 1], down),
            send(sv(nxt, h1).at, xa1.at, rs_s.at[k, 2], rs_r.at[k, 2], up),
            send(sv(prv, h0).at, xb0.at, rs_s.at[k, 3], rs_r.at[k, 3], down),
        ]
        second = [
            send(sv(nxt, h0).at, xa0.at, rs_s.at[k, 4], rs_r.at[k, 4], up),
            send(sv(prv, h1).at, xb1.at, rs_s.at[k, 5], rs_r.at[k, 5], down),
        ]

        def fold_first():
            add_views(sv(nxt, h0), [sv(nxt, h0), la_v], BF16)
            add_views(sv(prv, h1), [sv(prv, h1), lb_v], BF16)

        full = sv(mine, ALL)

        def fold_second():
            add_views(full, [full, own(xa, fs, nr, nc), own(xb, fs, nr, nc)], BF16)

        def uv(p2):
            return sv(mine, ("at", p2))

        us = uv(0).sizes
        l3_v = [own(l3.at[d], us, nr, nc) for d in range(3)]
        third = [
            send(uv(ring(a2, d)).at, l3_v[d - 1].at, rs_s.at[k, 5 + d], rs_r.at[k, 5 + d], device(**{a2: ring(a2, d)}))
            for d in (1, 2, 3)
        ]

        def fold_third():
            add_views(uv(me[a2]), [uv(me[a2])] + l3_v, BF16)

        def vv(p3):
            return sv(mine, ("at", me[a2]), ("at", p3))

        l4_v = [own(l4.at[d], [1, 1, 1, 1], nr, nc) for d in range(3)]
        fourth = [
            send(vv(ring(a3, d)).at, l4_v[d - 1].at, rs_s.at[k, 8 + d], rs_r.at[k, 8 + d], device(**{a3: ring(a3, d)}))
            for d in (1, 2, 3)
        ]

        def fold_fourth():
            zero = (0, 0, 0, 0)
            v = vv(me[a3])
            total = v.ref[v.index(zero)].astype(F32)
            for w in l4_v:
                total = total + w.ref[w.index(zero)].astype(F32)
            grad_ref[pl.ds(*rows), pl.ds(*cols)] = total

        return first, fold_first, second, fold_second, third, fold_third, fourth, fold_fourth

    plans = [rs(k) for k in colors]
    early = keep([c for p in plans for c in p[0][:2]])
    raw = keep([c for p in plans for c in p[0][2:]])
    second = keep([c for p in plans for c in p[2]])
    third = keep([c for p in plans for c in p[4]])
    fourth = keep([c for p in plans for c in p[6]])

    start(early)
    arrived(far)
    start(relay)
    start(dies[1])
    start(dies[3])
    start(raw)
    arrived(mv_x)
    start(mv_z)
    Z1[:, z] = X1[:, z]
    for p in plans:
        arrived(p[0][:2])
        p[1]()
        start(p[2])

    arrived(relay)
    start(dies[2])

    def slot(s):
        i = inv_ref[s]
        return (
            lax.div(i, 32), lax.rem(lax.div(i, 8), 4), lax.rem(lax.div(i, 4), 2), lax.rem(lax.div(i, 2), 2), lax.rem(i, 2),
        )

    def assemble(n, carry):
        j0 = pl.multiple_of(n * 16, 16)
        for h in range(2):
            slots = [slot(2 * (n * 16 + t) + h) for t in range(16)]
            for b0 in range(0, 128, 16):
                got = jnp.swapaxes(jnp.stack([G[i + (pl.ds(b0, 16), slice(None))] for i in slots], axis=0), 0, 1)
                for b in range(16):
                    W[b0 + b, pl.ds(j0, 16), pl.ds(256 * h, 256)] = got[b]
        return carry

    leave = [
        pltpu.make_async_copy(out_v.at[m % 2], out_hbm.at[pl.ds(256 * m, 256), :], out_sem.at[m]) for m in range(4)
    ]

    def project(m):
        rows = jnp.concatenate([tok[q, pl.ds(256 * m, 256), :] for q in range(32)], axis=1)
        if m >= 2:
            leave[m - 2].wait()
        out_v[m % 2] = jnp.dot(rows, W[...].reshape(D, KV), preferred_element_type=F32)
        leave[m].start()

    for d in (0, 1, 3, 2):
        arrived(dies[d])
    lax.fori_loop(0, 4, assemble, 0)
    project(0)
    for p in plans:
        arrived(p[0][2:] + p[2])
        p[3]()
        start(p[4])
    project(1)
    project(2)
    for p in plans:
        arrived(p[4])
        p[5]()
        start(p[6])
    project(3)

    arrived(mv_z)
    owner = jnp.dot(
        owner_vec[...].astype(F32).astype(BF16),
        one_hot(iota(sq, 0) == lax.rem(iota(sq, 1), 4) * 32 + iota(sq, 1) // 4),
        preferred_element_type=F32,
    )
    strips = Z1[...].reshape(128, 512)
    halves = [
        jnp.dot(
            one_hot(owner == (2 * iota((64, 128), 0) + h).astype(F32)), strips, preferred_element_type=F32
        ).astype(BF16)
        for h in range(2)
    ]
    for i in range(2):
        for h in range(2):
            m_ref[i, :, pl.ds(256 * h, 256)] = halves[h][:, 256 * i : 256 * i + 256]
    wrow_ref[...] = W[nown_ref[f] * 4 + r]
    for p in plans:
        arrived(p[6])
        p[7]()
    leave[2].wait()
    leave[3].wait()
    for c in everything:
        c.wait_send()


def landing_shapes():
    shapes = []
    at = ("at", 0)
    for (a1, a2, a3), rows, cols in RS_COLORS:
        n, m = rows[1], cols[1]

        def size(spec):
            return tuple(static_sizes(spec))

        half = size({a1: "at", a2: "half", a3: "all"}) + (n, m)
        full = size({a1: "at", a2: "all", a3: "all"}) + (n, m)
        line = size({a1: "at", a2: "at", a3: "all"}) + (n, m)
        shapes += [
            pltpu.VMEM(half, BF16), pltpu.VMEM(half, BF16),
            pltpu.VMEM(full, BF16), pltpu.VMEM(full, BF16),
            pltpu.VMEM((3,) + line, BF16), pltpu.VMEM((3, 1, 1, 1, 1, n, m), BF16),
        ]
    return shapes


def static_sizes(spec):
    sizes = []
    for axis in ("x", "z", "y"):
        kind = spec[axis]
        if axis == "y":
            sizes += {"at": [1, 1], "half": [1, 2], "all": [2, 2]}[kind]
        else:
            sizes += {"at": [1], "half": [2], "all": [4]}[kind]
    return sizes


def fused(new_owner, inverse, old_owner, tokens, cotangent, old_weight, old_first, old_second):
    smem = pl.BlockSpec(memory_space=pltpu.SMEM)
    vmem = pl.BlockSpec(memory_space=pltpu.VMEM)
    anywhere = pl.BlockSpec(memory_space=pl.ANY)
    dma = pltpu.SemaphoreType.DMA
    return pl.pallas_call(
        kernel,
        out_shape=(
            jax.ShapeDtypeStruct((ROWS, KV), F32),
            jax.ShapeDtypeStruct((64, KV), F32),
            jax.ShapeDtypeStruct((2, 64, KV), BF16),
            jax.ShapeDtypeStruct((64, KV), BF16),
        ),
        in_specs=[smem, smem, vmem, vmem] + [anywhere] * 4 + [vmem],
        out_specs=(anywhere, vmem, vmem, vmem),
        scratch_shapes=[
            pltpu.VMEM((ROWS, KV), BF16),
            pltpu.VMEM((64, KV), F32),
            pltpu.VMEM((64, KV), F32),
            pltpu.VMEM((2, 256, KV), F32),
            dma((3,)),
            dma((4,)),
            pltpu.VMEM((32, ROWS, 256), BF16),
            pltpu.VMEM((4, 4, 2, 2, 2, 128, 256), BF16),
            pltpu.VMEM((128, 64, KV), BF16),
            pltpu.VMEM((4, 4, 2, 2, 2, 64, KV), BF16),
            pltpu.VMEM((4, 4, 2, 2, 64, KV), BF16),
            pltpu.VMEM((4, 4, 2, 2, 64, KV), BF16),
            pltpu.VMEM((2, 2, 2, 16, 512), BF16),
            pltpu.VMEM((2, 2, 2, 16, 512), BF16),
            pltpu.VMEM((2, 2, 2, 16, 512), BF16),
            pltpu.VMEM((4, 4, 8, 512), BF16),
            pltpu.VMEM((4, 4, 8, 512), BF16),
            pltpu.VMEM((4, 4, 8, 512), BF16),
        ]
        + landing_shapes()
        + [
            dma((32,)),
            dma((3, 10)), dma((3, 10)), dma((3, 4)), dma((3, 4)),
            dma((4,)), dma((4,)), dma((3, 12)), dma((3, 12)),
            dma((10,)), dma((10,)),
        ],
        compiler_params=pltpu.CompilerParams(
            collective_id=0, has_side_effects=True, vmem_limit_bytes=67_000_000
        ),
        name="gather_grad_project",
    )(
        new_owner, inverse, new_owner.reshape(1, 32), old_owner.reshape(1, 128),
        tokens, cotangent, old_first, old_second, old_weight,
    )


def body(tokens, cotangent, old_weight, old_first, old_second, old_owner, new_owner):
    slot_ids = jnp.arange(128, dtype=jnp.int32)
    at = (slot_ids % 32) * 4 + slot_ids // 32
    inverse = jnp.sum(
        jnp.where(old_owner[None, :] == slot_ids[:, None], at[None, :], 0), axis=1
    ).astype(jnp.int32)
    projected, gradient, moments, weight_rows = fused(
        new_owner, inverse, old_owner, tokens, cotangent, old_weight, old_first, old_second
    )
    first_next = beta_one * moments[0].astype(F32) + (1.0 - beta_one) * gradient
    second_next = beta_two * moments[1].astype(F32) + (1.0 - beta_two) * gradient * gradient
    step_size = first_next / correction_one / (jnp.sqrt(second_next / correction_two) + epsilon)
    updated = (weight_rows.astype(F32) * (1.0 - learn_rate * decay_rate) - learn_rate * step_size).astype(BF16)
    return (projected.astype(BF16), updated, first_next, second_next)


def solution(mesh):
    rows = P(("rep", "fsdp"), None)
    return jax.shard_map(
        body,
        mesh=mesh,
        in_specs=(rows, rows, rows, rows, rows, P(), P()),
        out_specs=(rows, rows, rows, rows),
        check_vma=False,
    )
```

```python
import functools
import jax
import jax.numpy as jnp
from jax import lax
from jax.experimental import pallas as pl
from jax.experimental.pallas import tpu as pltpu
from jax.sharding import PartitionSpec as P

beta_one = 0.9
beta_two = 0.95
learn_rate = 0.001
decay_rate = 0.1
epsilon = 1e-08
correction_one = 1.0 - 0.9**10
correction_two = 1.0 - 0.95**10

MESH = pl.DeviceIdType.MESH
F32 = jnp.float32
BF16 = jnp.bfloat16
ROWS = 1024
D = 8192
KV = 512

RS_COLORS = (
    (("x", "y", "z"), (0, 48), (0, 256)),
    (("y", "z", "x"), (0, 48), (256, 256)),
    (("z", "x", "y"), (48, 16), (0, 512)),
)
AG_COLORS = (
    (("z", "y", "x"), (0, 48)),
    (("x", "z", "y"), (48, 48)),
    (("y", "x", "z"), (96, 32)),
)


def cut(spec):
    starts, sizes = [], []
    for axis in ("x", "z", "y"):
        kind, value = spec[axis]
        if axis == "y":
            if kind == "at":
                starts += [lax.rem(value, 2), value // 2]
                sizes += [1, 1]
            elif kind == "half":
                starts += [value, 0]
                sizes += [1, 2]
            else:
                starts += [0, 0]
                sizes += [2, 2]
        else:
            if kind == "at":
                starts.append(value)
                sizes.append(1)
            elif kind == "half":
                starts.append(2 * value)
                sizes.append(2)
            else:
                starts.append(0)
                sizes.append(4)
    return starts, sizes


ALL = ("all", 0)


class View:
    def __init__(self, ref, spec, rows, cols):
        self.ref, self.rows, self.cols = ref, rows, cols
        self.starts, self.sizes = cut(spec)

    @property
    def at(self):
        lead = tuple(pl.ds(s, n) for s, n in zip(self.starts, self.sizes))
        return self.ref.at[lead + (pl.ds(*self.rows), pl.ds(*self.cols))]

    def index(self, i):
        return tuple(s + k for s, k in zip(self.starts, i)) + (
            pl.ds(*self.rows),
            pl.ds(*self.cols),
        )


def own(ref, sizes, rows, cols, offset=(0, 0, 0, 0)):
    v = View.__new__(View)
    v.ref, v.rows, v.cols = ref, (0, rows), (0, cols)
    v.starts, v.sizes = list(offset), list(sizes)
    return v


def add_views(dst, sources, dtype):
    sizes = dst.sizes
    count = sizes[0] * sizes[1] * sizes[2] * sizes[3]

    def step(n, carry):
        i3 = lax.rem(n, sizes[3])
        n = lax.div(n, sizes[3])
        i2 = lax.rem(n, sizes[2])
        n = lax.div(n, sizes[2])
        i1 = lax.rem(n, sizes[1])
        i0 = lax.div(n, sizes[1])
        i = (i0, i1, i2, i3)
        total = sources[0].ref[sources[0].index(i)].astype(F32)
        for s in sources[1:]:
            total = total + s.ref[s.index(i)].astype(F32)
        dst.ref[dst.index(i)] = total.astype(dtype)
        return carry

    lax.fori_loop(0, count, step, 0)


def iota(shape, dim):
    return lax.broadcasted_iota(jnp.int32, shape, dim)


def one_hot(mask):
    return mask.astype(F32).astype(BF16)


def stack_halves(v):
    return jnp.concatenate([v[:, :256], v[:, 256:]], axis=0)


def kernel(
    nown_ref, nown_vec, owner_vec, tok_hbm, cot_hbm, first_hbm, second_hbm, w_ref,
    out_hbm, grad_ref, m_ref, wrow_ref,
    cot_ref, first_ref, second_ref, out_v, in_sem, out_sem, inv_vec, inv_ref, inv_sem,
    tok, G, W, part, recv, S,
    M0, C1, Y1, XZ, X1, Z1,
    *rest,
):
    (tok_sem, ag_s, ag_r, die_s, die_r, ex_s, ex_r, rs_s, rs_r, mv_s, mv_r) = rest[-11:]
    landing = (rest[0:6], rest[6:12], rest[12:18])
    r = lax.axis_index("rep")
    f = lax.axis_index("fsdp")
    yh, core = r // 2, lax.rem(r, 2)
    x, z, yl = f // 8, lax.rem(f // 2, 4), lax.rem(f, 2)
    me = {"x": x, "y": yh * 2 + yl, "z": z, "c": core}

    def device(**moved):
        p = dict(me, **moved)
        return ((p["y"] // 2) * 2 + p["c"], p["x"] * 8 + p["z"] * 2 + lax.rem(p["y"], 2))

    def ring(axis, d):
        return lax.rem(me[axis] + d, 4)

    def send(src, dst, ss, rs, to):
        return pltpu.make_async_remote_copy(
            src_ref=src, dst_ref=dst, send_sem=ss, recv_sem=rs, device_id=to, device_id_type=MESH
        )

    def start(copies):
        for c in copies:
            c.start()

    def arrived(copies):
        for c in copies:
            c.wait_recv()

    everything = []

    def keep(copies):
        everything.extend(copies)
        return copies

    barrier = pltpu.get_barrier_semaphore()
    for axis in ("x", "y", "z"):
        for d in (1, 2, 3):
            pl.semaphore_signal(barrier, inc=1, device_id=device(**{axis: ring(axis, d)}), device_id_type=MESH)
    partner = device(c=1 - core)
    pl.semaphore_signal(barrier, inc=1, device_id=partner, device_id_type=MESH)

    tok_copies = [
        pltpu.make_async_copy(tok_hbm.at[:, pl.ds(256 * q, 256)], tok.at[q], tok_sem.at[q])
        for q in range(32)
    ]
    in_copies = [
        pltpu.make_async_copy(a, b, in_sem.at[i])
        for i, (a, b) in enumerate(((first_hbm, first_ref), (second_hbm, second_ref), (cot_hbm, cot_ref)))
    ]
    start(in_copies)
    start(tok_copies)

    sq = (128, 128)
    split = one_hot(iota(sq, 1) == lax.rem(iota(sq, 0), 2) * 64 + iota(sq, 0) // 2)
    G[x, z, yl, yh, core] = jnp.dot(split, stack_halves(w_ref[...]), preferred_element_type=F32).astype(BF16)

    def gbox(spec, blocks):
        starts, sizes = cut(spec)
        lead = tuple(pl.ds(s, n) for s, n in zip(starts, sizes))
        return G.at[lead + (pl.ds(core, 1), pl.ds(*blocks), slice(None))]

    def ag_line(k):
        axes, blocks = AG_COLORS[k]
        a = axes[0]
        box = gbox({t: ("at", me[t]) for t in axes}, blocks)
        return [
            send(box, box, ag_s.at[k, d - 1], ag_r.at[k, d - 1], device(**{a: ring(a, d)}))
            for d in (1, 2, 3)
        ]

    def ag_plane(k):
        axes, blocks = AG_COLORS[k]
        a = axes[1]
        box = gbox({axes[0]: ALL, a: ("at", me[a]), axes[2]: ("at", me[axes[2]])}, blocks)
        return [
            send(box, box, ag_s.at[k, 2 + d], ag_r.at[k, 2 + d], device(**{a: ring(a, d)}))
            for d in (1, 2, 3)
        ]

    def ag_box(k, at, half=None):
        axes, blocks = AG_COLORS[k]
        first = ALL if half is None else ("half", half)
        return gbox({axes[0]: first, axes[1]: ALL, axes[2]: ("at", at)}, blocks)

    def ag_far(k):
        a = AG_COLORS[k][0][2]
        box = ag_box(k, me[a])
        return [
            send(box, box, ag_s.at[k, 6 + i], ag_r.at[k, 6 + i], device(**{a: ring(a, d)}))
            for i, d in enumerate((1, 3))
        ]

    def ag_relay(k):
        a = AG_COLORS[k][0][2]
        up = ag_box(k, ring(a, 3), 0)
        down = ag_box(k, ring(a, 1), 1)
        return [
            send(up, up, ag_s.at[k, 8], ag_r.at[k, 8], device(**{a: ring(a, 1)})),
            send(down, down, ag_s.at[k, 9], ag_r.at[k, 9], device(**{a: ring(a, 3)})),
        ]

    def die(k, d):
        a = AG_COLORS[k][0][2]
        box = ag_box(k, ring(a, d))
        return send(box, box, die_s.at[k, d], die_r.at[k, d], partner)

    colors = range(3)
    line = keep([c for k in colors for c in ag_line(k)])
    plane = keep([c for k in colors for c in ag_plane(k)])
    far = keep([c for k in colors for c in ag_far(k)])
    relay = keep([c for k in colors for c in ag_relay(k)])
    dies = [keep([die(k, d) for k in colors]) for d in range(4)]

    pl.semaphore_wait(barrier, 10)
    start(line)

    at = lax.rem(iota(sq, 1), 32) * 4 + iota(sq, 1) // 32
    column = jnp.max(jnp.where(owner_vec[...] == iota(sq, 0), at, 0), axis=1, keepdims=True)
    inv_vec[...] = jnp.max(jnp.where(iota(sq, 0) == iota(sq, 1), column, 0), axis=0, keepdims=True)
    inv_copy = pltpu.make_async_copy(inv_vec, inv_ref, inv_sem)

    d = iota(sq, 1)
    dc, dyl, dyh, dx, dz = d // 64, lax.rem(d // 32, 2), lax.rem(d // 16, 2), lax.rem(d // 4, 4), lax.rem(d, 4)
    pick = one_hot((iota(sq, 0) == dx * 8 + dz * 2 + dyl)[:32])
    block = 4.0 * jnp.dot(nown_vec[...].astype(F32).astype(BF16), pick, preferred_element_type=F32)
    block = block + (dyh * 2 + dc)[:1].astype(F32)
    sp = iota(sq, 0)
    choose = one_hot(block == (2 * lax.rem(sp, 64) + sp // 64).astype(F32))
    in_copies[0].wait()
    in_copies[1].wait()
    moments = jnp.concatenate(
        [stack_halves(first_ref[...].astype(BF16)), stack_halves(second_ref[...].astype(BF16))], axis=1
    )
    moved = lax.dot_general(choose, moments, (((0,), (0,)), ((), ())), preferred_element_type=F32).astype(BF16)
    for i in range(8):
        M0[i // 4, (i // 2) % 2, i % 2] = moved[16 * i : 16 * i + 16]

    mv_c = keep([send(M0.at[1 - core], C1.at[core], mv_s.at[0], mv_r.at[0], partner)])
    start(mv_c)
    C1[core] = M0[core]
    inv_copy.start()
    mv_y = keep([
        send(
            C1.at[:, lax.rem(ring("y", d), 2), ring("y", d) // 2], Y1.at[yl, yh],
            mv_s.at[d], mv_r.at[d], device(y=ring("y", d)),
        )
        for d in (1, 2, 3)
    ])
    mv_x = keep([
        send(XZ.at[ring("x", d)], X1.at[x], mv_s.at[3 + d], mv_r.at[3 + d], device(x=ring("x", d)))
        for d in (1, 2, 3)
    ])
    mv_z = keep([
        send(X1.at[:, ring("z", d)], Z1.at[:, z], mv_s.at[6 + d], mv_r.at[6 + d], device(z=ring("z", d)))
        for d in (1, 2, 3)
    ])

    arrived(line)
    start(plane)
    in_copies[2].wait()
    for c in tok_copies:
        c.wait()

    def grad_step(n, carry):
        g = lax.div(n, 8)
        m = lax.rem(n, 8)
        block = lax.dot_general(
            tok[nown_ref[n]], cot_ref[...], (((0,), (0,)), ((), ())), preferred_element_type=F32
        ).astype(BF16)
        for i in range(4):
            part[g, lax.div(m, 2), lax.rem(m, 2), i // 2, i % 2] = block[64 * i : 64 * i + 64]
        return carry

    exchange = keep([
        send(part.at[g, :, :, :, 1 - core], recv.at[g], ex_s.at[g], ex_r.at[g], partner)
        for g in range(4)
    ])

    def gradient(lo, hi):
        lax.fori_loop(lo, hi, grad_step, 0, unroll=8)

    gradient(0, 8)
    exchange[0].start()
    arrived(mv_c)
    start(mv_y)
    Y1[yl, yh] = C1[:, yl, yh]
    gradient(8, 16)
    exchange[1].start()
    arrived(plane)
    start(far)
    start(dies[0])
    gradient(16, 24)
    exchange[2].start()
    arrived(mv_y)
    rows = Y1[...].reshape(128, 512)
    swap = one_hot(iota(sq, 1) == lax.rem(iota(sq, 0), 8) * 16 + iota(sq, 0) // 8)
    XZ[...] = jnp.dot(swap, rows, preferred_element_type=F32).astype(BF16).reshape(4, 4, 8, 512)
    start(mv_x)
    X1[x] = XZ[x]
    gradient(24, 32)
    exchange[3].start()

    def chip_sum(g):
        exchange[g].wait_recv()

        def step(n, carry):
            i3 = lax.rem(n, 2)
            i2 = lax.rem(lax.div(n, 2), 2)
            i1 = lax.div(n, 4)
            S[g, i1, i2, i3] = (
                part[g, i1, i2, i3, core].astype(F32) + recv[g, i1, i2, i3].astype(F32)
            ).astype(BF16)
            return carry

        lax.fori_loop(0, 16, step, 0)

    for g in range(4):
        chip_sum(g)

    def rs(k):
        (a1, a2, a3), rows, cols = RS_COLORS[k]
        la, lb, xa, xb, l3, l4 = landing[k]
        up, down = device(**{a1: ring(a1, 1)}), device(**{a1: ring(a1, 3)})

        def sv(p1, s2, s3=ALL):
            return View(S, {a1: ("at", p1), a2: s2, a3: s3}, rows, cols)

        h0, h1 = ("half", 0), ("half", 1)
        mine, nxt, prv, opp = me[a1], ring(a1, 1), ring(a1, 3), ring(a1, 2)
        hs = sv(opp, h0).sizes
        fs = sv(opp, ALL).sizes
        hoff = [0 if p == q else p for p, q in zip(hs, fs)]
        nr, nc = rows[1], cols[1]
        la_v, lb_v = own(la, hs, nr, nc), own(lb, hs, nr, nc)
        xa0, xa1 = own(xa, hs, nr, nc), own(xa, hs, nr, nc, hoff)
        xb0, xb1 = own(xb, hs, nr, nc), own(xb, hs, nr, nc, hoff)
        first = [
            send(sv(opp, h0).at, la_v.at, rs_s.at[k, 0], rs_r.at[k, 0], up),
            send(sv(opp, h1).at, lb_v.at, rs_s.at[k, 1], rs_r.at[k, 1], down),
            send(sv(nxt, h1).at, xa1.at, rs_s.at[k, 2], rs_r.at[k, 2], up),
            send(sv(prv, h0).at, xb0.at, rs_s.at[k, 3], rs_r.at[k, 3], down),
        ]
        second = [
            send(sv(nxt, h0).at, xa0.at, rs_s.at[k, 4], rs_r.at[k, 4], up),
            send(sv(prv, h1).at, xb1.at, rs_s.at[k, 5], rs_r.at[k, 5], down),
        ]

        def fold_first():
            add_views(sv(nxt, h0), [sv(nxt, h0), la_v], BF16)
            add_views(sv(prv, h1), [sv(prv, h1), lb_v], BF16)

        full = sv(mine, ALL)

        def fold_second():
            add_views(full, [full, own(xa, fs, nr, nc), own(xb, fs, nr, nc)], BF16)

        def uv(p2):
            return sv(mine, ("at", p2))

        us = uv(0).sizes
        l3_v = [own(l3.at[d], us, nr, nc) for d in range(3)]
        third = [
            send(uv(ring(a2, d)).at, l3_v[d - 1].at, rs_s.at[k, 5 + d], rs_r.at[k, 5 + d], device(**{a2: ring(a2, d)}))
            for d in (1, 2, 3)
        ]

        def fold_third():
            add_views(uv(me[a2]), [uv(me[a2])] + l3_v, BF16)

        def vv(p3):
            return sv(mine, ("at", me[a2]), ("at", p3))

        l4_v = [own(l4.at[d], [1, 1, 1, 1], nr, nc) for d in range(3)]
        fourth = [
            send(vv(ring(a3, d)).at, l4_v[d - 1].at, rs_s.at[k, 8 + d], rs_r.at[k, 8 + d], device(**{a3: ring(a3, d)}))
            for d in (1, 2, 3)
        ]

        def fold_fourth():
            zero = (0, 0, 0, 0)
            v = vv(me[a3])
            total = v.ref[v.index(zero)].astype(F32)
            for w in l4_v:
                total = total + w.ref[w.index(zero)].astype(F32)
            grad_ref[pl.ds(*rows), pl.ds(*cols)] = total

        return first, fold_first, second, fold_second, third, fold_third, fourth, fold_fourth

    plans = [rs(k) for k in colors]
    early = keep([c for p in plans for c in p[0][:2]])
    raw = keep([c for p in plans for c in p[0][2:]])
    second = keep([c for p in plans for c in p[2]])
    third = keep([c for p in plans for c in p[4]])
    fourth = keep([c for p in plans for c in p[6]])

    start(early)
    arrived(far)
    start(relay)
    start(dies[1])
    start(dies[3])
    start(raw)
    arrived(mv_x)
    start(mv_z)
    Z1[:, z] = X1[:, z]
    for p in plans:
        arrived(p[0][:2])
        p[1]()
        start(p[2])

    arrived(relay)
    start(dies[2])

    def slot(s):
        i = inv_ref[0, s]
        return (
            lax.div(i, 32), lax.rem(lax.div(i, 8), 4), lax.rem(lax.div(i, 4), 2), lax.rem(lax.div(i, 2), 2), lax.rem(i, 2),
        )

    def assemble(n, carry):
        j0 = pl.multiple_of(n * 16, 16)
        for h in range(2):
            slots = [slot(2 * (n * 16 + t) + h) for t in range(16)]
            for b0 in range(0, 128, 16):
                got = jnp.swapaxes(jnp.stack([G[i + (pl.ds(b0, 16), slice(None))] for i in slots], axis=0), 0, 1)
                for b in range(16):
                    W[b0 + b, pl.ds(j0, 16), pl.ds(256 * h, 256)] = got[b]
        return carry

    leave = [
        pltpu.make_async_copy(out_v.at[m % 2], out_hbm.at[pl.ds(256 * m, 256), :], out_sem.at[m]) for m in range(4)
    ]

    def project(m):
        rows = jnp.concatenate([tok[q, pl.ds(256 * m, 256), :] for q in range(32)], axis=1)
        if m >= 2:
            leave[m - 2].wait()
        out_v[m % 2] = jnp.dot(rows, W[...].reshape(D, KV), preferred_element_type=F32).astype(BF16)
        leave[m].start()

    for d in (0, 1, 3, 2):
        arrived(dies[d])
    inv_copy.wait()
    lax.fori_loop(0, 4, assemble, 0)
    project(0)
    for p in plans:
        arrived(p[0][2:] + p[2])
        p[3]()
        start(p[4])
    project(1)
    project(2)
    for p in plans:
        arrived(p[4])
        p[5]()
        start(p[6])
    project(3)

    arrived(mv_z)
    owner = jnp.dot(
        owner_vec[...].astype(F32).astype(BF16),
        one_hot(iota(sq, 0) == lax.rem(iota(sq, 1), 4) * 32 + iota(sq, 1) // 4),
        preferred_element_type=F32,
    )
    strips = Z1[...].reshape(128, 512)
    halves = [
        jnp.dot(
            one_hot(owner == (2 * iota((64, 128), 0) + h).astype(F32)), strips, preferred_element_type=F32
        ).astype(BF16)
        for h in range(2)
    ]
    for i in range(2):
        for h in range(2):
            m_ref[i, :, pl.ds(256 * h, 256)] = halves[h][:, 256 * i : 256 * i + 256]
    wrow_ref[...] = W[nown_ref[f] * 4 + r]
    for p in plans:
        arrived(p[6])
        p[7]()
    leave[2].wait()
    leave[3].wait()
    for c in everything:
        c.wait_send()


def landing_shapes():
    shapes = []
    at = ("at", 0)
    for (a1, a2, a3), rows, cols in RS_COLORS:
        n, m = rows[1], cols[1]

        def size(spec):
            return tuple(static_sizes(spec))

        half = size({a1: "at", a2: "half", a3: "all"}) + (n, m)
        full = size({a1: "at", a2: "all", a3: "all"}) + (n, m)
        line = size({a1: "at", a2: "at", a3: "all"}) + (n, m)
        shapes += [
            pltpu.VMEM(half, BF16), pltpu.VMEM(half, BF16),
            pltpu.VMEM(full, BF16), pltpu.VMEM(full, BF16),
            pltpu.VMEM((3,) + line, BF16), pltpu.VMEM((3, 1, 1, 1, 1, n, m), BF16),
        ]
    return shapes


def static_sizes(spec):
    sizes = []
    for axis in ("x", "z", "y"):
        kind = spec[axis]
        if axis == "y":
            sizes += {"at": [1, 1], "half": [1, 2], "all": [2, 2]}[kind]
        else:
            sizes += {"at": [1], "half": [2], "all": [4]}[kind]
    return sizes


def fused(new_owner, old_owner, tokens, cotangent, old_weight, old_first, old_second):
    smem = pl.BlockSpec(memory_space=pltpu.SMEM)
    vmem = pl.BlockSpec(memory_space=pltpu.VMEM)
    anywhere = pl.BlockSpec(memory_space=pl.ANY)
    dma = pltpu.SemaphoreType.DMA
    return pl.pallas_call(
        kernel,
        out_shape=(
            jax.ShapeDtypeStruct((ROWS, KV), BF16),
            jax.ShapeDtypeStruct((64, KV), F32),
            jax.ShapeDtypeStruct((2, 64, KV), BF16),
            jax.ShapeDtypeStruct((64, KV), BF16),
        ),
        in_specs=[smem, vmem, vmem] + [anywhere] * 4 + [vmem],
        out_specs=(anywhere, vmem, vmem, vmem),
        scratch_shapes=[
            pltpu.VMEM((ROWS, KV), BF16),
            pltpu.VMEM((64, KV), F32),
            pltpu.VMEM((64, KV), F32),
            pltpu.VMEM((2, 256, KV), BF16),
            dma((3,)),
            dma((4,)),
            pltpu.VMEM((1, 128), jnp.int32),
            pltpu.SMEM((1, 128), jnp.int32),
            dma,
            pltpu.VMEM((32, ROWS, 256), BF16),
            pltpu.VMEM((4, 4, 2, 2, 2, 128, 256), BF16),
            pltpu.VMEM((128, 64, KV), BF16),
            pltpu.VMEM((4, 4, 2, 2, 2, 64, KV), BF16),
            pltpu.VMEM((4, 4, 2, 2, 64, KV), BF16),
            pltpu.VMEM((4, 4, 2, 2, 64, KV), BF16),
            pltpu.VMEM((2, 2, 2, 16, 512), BF16),
            pltpu.VMEM((2, 2, 2, 16, 512), BF16),
            pltpu.VMEM((2, 2, 2, 16, 512), BF16),
            pltpu.VMEM((4, 4, 8, 512), BF16),
            pltpu.VMEM((4, 4, 8, 512), BF16),
            pltpu.VMEM((4, 4, 8, 512), BF16),
        ]
        + landing_shapes()
        + [
            dma((32,)),
            dma((3, 10)), dma((3, 10)), dma((3, 4)), dma((3, 4)),
            dma((4,)), dma((4,)), dma((3, 12)), dma((3, 12)),
            dma((10,)), dma((10,)),
        ],
        compiler_params=pltpu.CompilerParams(
            collective_id=0, has_side_effects=True, vmem_limit_bytes=67_000_000
        ),
        name="gather_grad_project",
    )(
        new_owner, new_owner.reshape(1, 32), old_owner.reshape(1, 128),
        tokens, cotangent, old_first, old_second, old_weight,
    )


def finish_kernel(
    proj_hbm, grad_hbm, m_hbm, w_hbm, out_hbm, new_w_hbm, new_f_hbm, new_s_hbm,
    proj, grad, m, w, new_w, new_f, new_s, in_sem, out_sem,
):
    tiles = [pl.ds(256 * i, 256) for i in range(4)]
    small = [
        pltpu.make_async_copy(a, b, in_sem.at[i])
        for i, (a, b) in enumerate(((grad_hbm, grad), (m_hbm, m), (w_hbm, w)))
    ]
    enter = [pltpu.make_async_copy(proj_hbm.at[t], proj.at[t], in_sem.at[3 + i]) for i, t in enumerate(tiles)]
    leave = [pltpu.make_async_copy(proj.at[t], out_hbm.at[t], out_sem.at[3 + i]) for i, t in enumerate(tiles)]
    results = [
        pltpu.make_async_copy(a, b, out_sem.at[i])
        for i, (a, b) in enumerate(((new_w, new_w_hbm), (new_f, new_f_hbm), (new_s, new_s_hbm)))
    ]
    for c in small + enter:
        c.start()
    for c in small:
        c.wait()
    gradient = grad[...]
    first_next = beta_one * m[0].astype(F32) + (1.0 - beta_one) * gradient
    second_next = beta_two * m[1].astype(F32) + (1.0 - beta_two) * gradient * gradient
    step_size = first_next / correction_one / (jnp.sqrt(second_next / correction_two) + epsilon)
    new_f[...] = first_next
    new_s[...] = second_next
    new_w[...] = (w[...].astype(F32) * (1.0 - learn_rate * decay_rate) - learn_rate * step_size).astype(BF16)
    for a, b in zip(enter, leave):
        a.wait()
        b.start()
    for c in results:
        c.start()
    for c in results + leave:
        c.wait()


def finish(projected, gradient, moments, weight_rows):
    anywhere = pl.BlockSpec(memory_space=pl.ANY)
    f32, bf16 = pltpu.VMEM((64, KV), F32), pltpu.VMEM((64, KV), BF16)
    return pl.pallas_call(
        finish_kernel,
        out_shape=(
            jax.ShapeDtypeStruct((ROWS, KV), BF16),
            jax.ShapeDtypeStruct((64, KV), BF16),
            jax.ShapeDtypeStruct((64, KV), F32),
            jax.ShapeDtypeStruct((64, KV), F32),
        ),
        in_specs=[anywhere] * 4,
        out_specs=(anywhere,) * 4,
        scratch_shapes=[
            pltpu.VMEM((ROWS, KV), BF16), f32, pltpu.VMEM((2, 64, KV), BF16), bf16, bf16, f32, f32,
            pltpu.SemaphoreType.DMA((7,)), pltpu.SemaphoreType.DMA((7,)),
        ],
        name="adamw",
    )(projected, gradient, moments, weight_rows)


def body(tokens, cotangent, old_weight, old_first, old_second, old_owner, new_owner):
    projected, gradient, moments, weight_rows = fused(
        new_owner, old_owner, tokens, cotangent, old_weight, old_first, old_second
    )
    return finish(projected, gradient, moments, weight_rows)


def solution(mesh):
    rows = P(("rep", "fsdp"), None)
    return jax.shard_map(
        body,
        mesh=mesh,
        in_specs=(rows, rows, rows, rows, rows, P(), P()),
        out_specs=(rows, rows, rows, rows),
        check_vma=False,
    )
```

```python
import functools
import jax
import jax.numpy as jnp
from jax import lax
from jax.experimental import pallas as pl
from jax.experimental.pallas import tpu as pltpu
from jax.sharding import PartitionSpec as P

beta_one = 0.9
beta_two = 0.95
learn_rate = 0.001
decay_rate = 0.1
epsilon = 1e-08
correction_one = 1.0 - 0.9**10
correction_two = 1.0 - 0.95**10

MESH = pl.DeviceIdType.MESH
F32 = jnp.float32
BF16 = jnp.bfloat16
ROWS = 1024
D = 8192
KV = 512

RS_COLORS = (
    (("x", "y", "z"), (0, 48), (0, 256)),
    (("y", "z", "x"), (0, 48), (256, 256)),
    (("z", "x", "y"), (48, 16), (0, 512)),
)
AG_COLORS = (
    (("z", "y", "x"), (0, 48)),
    (("x", "z", "y"), (48, 48)),
    (("y", "x", "z"), (96, 32)),
)


def cut(spec):
    starts, sizes = [], []
    for axis in ("x", "z", "y"):
        kind, value = spec[axis]
        if axis == "y":
            if kind == "at":
                starts += [lax.rem(value, 2), value // 2]
                sizes += [1, 1]
            elif kind == "half":
                starts += [value, 0]
                sizes += [1, 2]
            else:
                starts += [0, 0]
                sizes += [2, 2]
        else:
            if kind == "at":
                starts.append(value)
                sizes.append(1)
            elif kind == "half":
                starts.append(2 * value)
                sizes.append(2)
            else:
                starts.append(0)
                sizes.append(4)
    return starts, sizes


ALL = ("all", 0)


class View:
    def __init__(self, ref, spec, rows, cols):
        self.ref, self.rows, self.cols = ref, rows, cols
        self.starts, self.sizes = cut(spec)

    @property
    def at(self):
        lead = tuple(pl.ds(s, n) for s, n in zip(self.starts, self.sizes))
        return self.ref.at[lead + (pl.ds(*self.rows), pl.ds(*self.cols))]

    def index(self, i):
        return tuple(s + k for s, k in zip(self.starts, i)) + (
            pl.ds(*self.rows),
            pl.ds(*self.cols),
        )


def own(ref, sizes, rows, cols, offset=(0, 0, 0, 0)):
    v = View.__new__(View)
    v.ref, v.rows, v.cols = ref, (0, rows), (0, cols)
    v.starts, v.sizes = list(offset), list(sizes)
    return v


def add_views(dst, sources, dtype):
    sizes = dst.sizes
    count = sizes[0] * sizes[1] * sizes[2] * sizes[3]

    def step(n, carry):
        i3 = lax.rem(n, sizes[3])
        n = lax.div(n, sizes[3])
        i2 = lax.rem(n, sizes[2])
        n = lax.div(n, sizes[2])
        i1 = lax.rem(n, sizes[1])
        i0 = lax.div(n, sizes[1])
        i = (i0, i1, i2, i3)
        total = sources[0].ref[sources[0].index(i)].astype(F32)
        for s in sources[1:]:
            total = total + s.ref[s.index(i)].astype(F32)
        dst.ref[dst.index(i)] = total.astype(dtype)
        return carry

    lax.fori_loop(0, count, step, 0)


def iota(shape, dim):
    return lax.broadcasted_iota(jnp.int32, shape, dim)


def one_hot(mask):
    return mask.astype(F32).astype(BF16)


def stack_halves(v):
    return jnp.concatenate([v[:, :256], v[:, 256:]], axis=0)


def kernel(
    nown_ref, nown_vec, owner_vec, tok_hbm, cot_hbm, first_hbm, second_hbm, w_ref,
    out_hbm, grad_ref, m_ref, wrow_ref,
    cot_ref, first_ref, second_ref, out_v, in_sem, out_sem, inv_vec, inv_ref, inv_sem,
    tok_a, tok_b, acc, G, W, part, recv, S,
    M0, C1, Y1, XZ, X1, Z1,
    *rest,
):
    (tok_sem, ag_s, ag_r, die_s, die_r, ex_s, ex_r, rs_s, rs_r, mv_s, mv_r) = rest[-11:]
    landing = (rest[0:6], rest[6:12], rest[12:18])
    r = lax.axis_index("rep")
    f = lax.axis_index("fsdp")
    yh, core = r // 2, lax.rem(r, 2)
    x, z, yl = f // 8, lax.rem(f // 2, 4), lax.rem(f, 2)
    me = {"x": x, "y": yh * 2 + yl, "z": z, "c": core}

    def device(**moved):
        p = dict(me, **moved)
        return ((p["y"] // 2) * 2 + p["c"], p["x"] * 8 + p["z"] * 2 + lax.rem(p["y"], 2))

    def ring(axis, d):
        return lax.rem(me[axis] + d, 4)

    def send(src, dst, ss, rs, to):
        return pltpu.make_async_remote_copy(
            src_ref=src, dst_ref=dst, send_sem=ss, recv_sem=rs, device_id=to, device_id_type=MESH
        )

    def start(copies):
        for c in copies:
            c.start()

    def arrived(copies):
        for c in copies:
            c.wait_recv()

    everything = []

    def keep(copies):
        everything.extend(copies)
        return copies

    barrier = pltpu.get_barrier_semaphore()
    for axis in ("x", "y", "z"):
        for d in (1, 2, 3):
            pl.semaphore_signal(barrier, inc=1, device_id=device(**{axis: ring(axis, d)}), device_id_type=MESH)
    partner = device(c=1 - core)
    pl.semaphore_signal(barrier, inc=1, device_id=partner, device_id_type=MESH)

    tok_copies = [
        pltpu.make_async_copy(
            tok_hbm.at[pl.ds(512 * h, 512), pl.ds(256 * q, 256)], tok.at[q], tok_sem.at[32 * h + q]
        )
        for h, tok in enumerate((tok_a, tok_b))
        for q in range(32)
    ]
    in_copies = [
        pltpu.make_async_copy(a, b, in_sem.at[i])
        for i, (a, b) in enumerate(((first_hbm, first_ref), (second_hbm, second_ref), (cot_hbm, cot_ref)))
    ]
    start(in_copies)
    start(tok_copies)

    sq = (128, 128)
    split = one_hot(iota(sq, 1) == lax.rem(iota(sq, 0), 2) * 64 + iota(sq, 0) // 2)
    G[x, z, yl, yh, core] = jnp.dot(split, stack_halves(w_ref[...]), preferred_element_type=F32).astype(BF16)

    def gbox(spec, blocks):
        starts, sizes = cut(spec)
        lead = tuple(pl.ds(s, n) for s, n in zip(starts, sizes))
        return G.at[lead + (pl.ds(core, 1), pl.ds(*blocks), slice(None))]

    def ag_line(k):
        axes, blocks = AG_COLORS[k]
        a = axes[0]
        box = gbox({t: ("at", me[t]) for t in axes}, blocks)
        return [
            send(box, box, ag_s.at[k, d - 1], ag_r.at[k, d - 1], device(**{a: ring(a, d)}))
            for d in (1, 2, 3)
        ]

    def ag_plane(k):
        axes, blocks = AG_COLORS[k]
        a = axes[1]
        box = gbox({axes[0]: ALL, a: ("at", me[a]), axes[2]: ("at", me[axes[2]])}, blocks)
        return [
            send(box, box, ag_s.at[k, 2 + d], ag_r.at[k, 2 + d], device(**{a: ring(a, d)}))
            for d in (1, 2, 3)
        ]

    def ag_box(k, at, half=None):
        axes, blocks = AG_COLORS[k]
        first = ALL if half is None else ("half", half)
        return gbox({axes[0]: first, axes[1]: ALL, axes[2]: ("at", at)}, blocks)

    def ag_far(k):
        a = AG_COLORS[k][0][2]
        box = ag_box(k, me[a])
        return [
            send(box, box, ag_s.at[k, 6 + i], ag_r.at[k, 6 + i], device(**{a: ring(a, d)}))
            for i, d in enumerate((1, 3))
        ]

    def ag_relay(k):
        a = AG_COLORS[k][0][2]
        up = ag_box(k, ring(a, 3), 0)
        down = ag_box(k, ring(a, 1), 1)
        return [
            send(up, up, ag_s.at[k, 8], ag_r.at[k, 8], device(**{a: ring(a, 1)})),
            send(down, down, ag_s.at[k, 9], ag_r.at[k, 9], device(**{a: ring(a, 3)})),
        ]

    def die(k, d):
        a = AG_COLORS[k][0][2]
        box = ag_box(k, ring(a, d))
        return send(box, box, die_s.at[k, d], die_r.at[k, d], partner)

    colors = range(3)
    line = keep([c for k in colors for c in ag_line(k)])
    plane = keep([c for k in colors for c in ag_plane(k)])
    far = keep([c for k in colors for c in ag_far(k)])
    relay = keep([c for k in colors for c in ag_relay(k)])
    dies = [keep([die(k, d) for k in colors]) for d in range(4)]

    pl.semaphore_wait(barrier, 10)
    start(line)

    at = lax.rem(iota(sq, 1), 32) * 4 + iota(sq, 1) // 32
    column = jnp.max(jnp.where(owner_vec[...] == iota(sq, 0), at, 0), axis=1, keepdims=True)
    inv_vec[...] = jnp.max(jnp.where(iota(sq, 0) == iota(sq, 1), column, 0), axis=0, keepdims=True)
    inv_copy = pltpu.make_async_copy(inv_vec, inv_ref, inv_sem)

    d = iota(sq, 1)
    dc, dyl, dyh, dx, dz = d // 64, lax.rem(d // 32, 2), lax.rem(d // 16, 2), lax.rem(d // 4, 4), lax.rem(d, 4)
    pick = one_hot((iota(sq, 0) == dx * 8 + dz * 2 + dyl)[:32])
    block = 4.0 * jnp.dot(nown_vec[...].astype(F32).astype(BF16), pick, preferred_element_type=F32)
    block = block + (dyh * 2 + dc)[:1].astype(F32)
    sp = iota(sq, 0)
    choose = one_hot(block == (2 * lax.rem(sp, 64) + sp // 64).astype(F32))
    in_copies[0].wait()
    in_copies[1].wait()
    moments = jnp.concatenate(
        [stack_halves(first_ref[...].astype(BF16)), stack_halves(second_ref[...].astype(BF16))], axis=1
    )
    moved = lax.dot_general(choose, moments, (((0,), (0,)), ((), ())), preferred_element_type=F32).astype(BF16)
    for i in range(8):
        M0[i // 4, (i // 2) % 2, i % 2] = moved[16 * i : 16 * i + 16]

    mv_c = keep([send(M0.at[1 - core], C1.at[core], mv_s.at[0], mv_r.at[0], partner)])
    start(mv_c)
    C1[core] = M0[core]
    inv_copy.start()
    mv_y = keep([
        send(
            C1.at[:, lax.rem(ring("y", d), 2), ring("y", d) // 2], Y1.at[yl, yh],
            mv_s.at[d], mv_r.at[d], device(y=ring("y", d)),
        )
        for d in (1, 2, 3)
    ])
    mv_x = keep([
        send(XZ.at[ring("x", d)], X1.at[x], mv_s.at[3 + d], mv_r.at[3 + d], device(x=ring("x", d)))
        for d in (1, 2, 3)
    ])
    mv_z = keep([
        send(X1.at[:, ring("z", d)], Z1.at[:, z], mv_s.at[6 + d], mv_r.at[6 + d], device(z=ring("z", d)))
        for d in (1, 2, 3)
    ])

    arrived(line)
    start(plane)
    in_copies[2].wait()
    for c in tok_copies[:32]:
        c.wait()

    def leave_block(n, g, m, block, carry):
        block = block.astype(BF16)
        for i in range(4):
            part[g, lax.div(m, 2), lax.rem(m, 2), i // 2, i % 2] = block[64 * i : 64 * i + 64]
        return carry

    def contract(a, b):
        return lax.dot_general(a, b, (((0,), (0,)), ((), ())), preferred_element_type=F32)

    def grad_begin(n, carry):
        acc[n] = contract(tok_a[nown_ref[n]], cot_ref[:512])
        return carry

    def grad_end(n, carry):
        block = acc[n] + contract(tok_b[nown_ref[n]], cot_ref[512:])
        return leave_block(n, 0, n, block, carry)

    def grad_step(n, carry):
        g = lax.div(n, 8)
        m = lax.rem(n, 8)
        both = jnp.concatenate([tok_a[nown_ref[n]], tok_b[nown_ref[n]]], axis=0)
        return leave_block(n, g, m, contract(both, cot_ref[...]), carry)

    exchange = keep([
        send(part.at[g, :, :, :, 1 - core], recv.at[g], ex_s.at[g], ex_r.at[g], partner)
        for g in range(4)
    ])

    def gradient(lo, hi):
        lax.fori_loop(lo, hi, grad_step, 0, unroll=8)

    lax.fori_loop(0, 8, grad_begin, 0, unroll=8)
    for c in tok_copies[32:]:
        c.wait()
    lax.fori_loop(0, 8, grad_end, 0, unroll=8)
    exchange[0].start()
    arrived(mv_c)
    start(mv_y)
    Y1[yl, yh] = C1[:, yl, yh]
    gradient(8, 16)
    exchange[1].start()
    arrived(plane)
    start(far)
    start(dies[0])
    gradient(16, 24)
    exchange[2].start()
    arrived(mv_y)
    rows = Y1[...].reshape(128, 512)
    swap = one_hot(iota(sq, 1) == lax.rem(iota(sq, 0), 8) * 16 + iota(sq, 0) // 8)
    XZ[...] = jnp.dot(swap, rows, preferred_element_type=F32).astype(BF16).reshape(4, 4, 8, 512)
    start(mv_x)
    X1[x] = XZ[x]
    gradient(24, 32)
    exchange[3].start()

    def chip_sum(g):
        exchange[g].wait_recv()

        def step(n, carry):
            i3 = lax.rem(n, 2)
            i2 = lax.rem(lax.div(n, 2), 2)
            i1 = lax.div(n, 4)
            S[g, i1, i2, i3] = (
                part[g, i1, i2, i3, core].astype(F32) + recv[g, i1, i2, i3].astype(F32)
            ).astype(BF16)
            return carry

        lax.fori_loop(0, 16, step, 0)

    for g in range(4):
        chip_sum(g)

    def rs(k):
        (a1, a2, a3), rows, cols = RS_COLORS[k]
        la, lb, xa, xb, l3, l4 = landing[k]
        up, down = device(**{a1: ring(a1, 1)}), device(**{a1: ring(a1, 3)})

        def sv(p1, s2, s3=ALL):
            return View(S, {a1: ("at", p1), a2: s2, a3: s3}, rows, cols)

        h0, h1 = ("half", 0), ("half", 1)
        mine, nxt, prv, opp = me[a1], ring(a1, 1), ring(a1, 3), ring(a1, 2)
        hs = sv(opp, h0).sizes
        fs = sv(opp, ALL).sizes
        hoff = [0 if p == q else p for p, q in zip(hs, fs)]
        nr, nc = rows[1], cols[1]
        la_v, lb_v = own(la, hs, nr, nc), own(lb, hs, nr, nc)
        xa0, xa1 = own(xa, hs, nr, nc), own(xa, hs, nr, nc, hoff)
        xb0, xb1 = own(xb, hs, nr, nc), own(xb, hs, nr, nc, hoff)
        first = [
            send(sv(opp, h0).at, la_v.at, rs_s.at[k, 0], rs_r.at[k, 0], up),
            send(sv(opp, h1).at, lb_v.at, rs_s.at[k, 1], rs_r.at[k, 1], down),
            send(sv(nxt, h1).at, xa1.at, rs_s.at[k, 2], rs_r.at[k, 2], up),
            send(sv(prv, h0).at, xb0.at, rs_s.at[k, 3], rs_r.at[k, 3], down),
        ]
        second = [
            send(sv(nxt, h0).at, xa0.at, rs_s.at[k, 4], rs_r.at[k, 4], up),
            send(sv(prv, h1).at, xb1.at, rs_s.at[k, 5], rs_r.at[k, 5], down),
        ]

        def fold_first():
            add_views(sv(nxt, h0), [sv(nxt, h0), la_v], BF16)
            add_views(sv(prv, h1), [sv(prv, h1), lb_v], BF16)

        full = sv(mine, ALL)

        def fold_second():
            add_views(full, [full, own(xa, fs, nr, nc), own(xb, fs, nr, nc)], BF16)

        def uv(p2):
            return sv(mine, ("at", p2))

        us = uv(0).sizes
        l3_v = [own(l3.at[d], us, nr, nc) for d in range(3)]
        third = [
            send(uv(ring(a2, d)).at, l3_v[d - 1].at, rs_s.at[k, 5 + d], rs_r.at[k, 5 + d], device(**{a2: ring(a2, d)}))
            for d in (1, 2, 3)
        ]

        def fold_third():
            add_views(uv(me[a2]), [uv(me[a2])] + l3_v, BF16)

        def vv(p3):
            return sv(mine, ("at", me[a2]), ("at", p3))

        l4_v = [own(l4.at[d], [1, 1, 1, 1], nr, nc) for d in range(3)]
        fourth = [
            send(vv(ring(a3, d)).at, l4_v[d - 1].at, rs_s.at[k, 8 + d], rs_r.at[k, 8 + d], device(**{a3: ring(a3, d)}))
            for d in (1, 2, 3)
        ]

        def fold_fourth():
            zero = (0, 0, 0, 0)
            v = vv(me[a3])
            total = v.ref[v.index(zero)].astype(F32)
            for w in l4_v:
                total = total + w.ref[w.index(zero)].astype(F32)
            grad_ref[pl.ds(*rows), pl.ds(*cols)] = total

        return first, fold_first, second, fold_second, third, fold_third, fourth, fold_fourth

    plans = [rs(k) for k in colors]
    early = keep([c for p in plans for c in p[0][:2]])
    raw = keep([c for p in plans for c in p[0][2:]])
    second = keep([c for p in plans for c in p[2]])
    third = keep([c for p in plans for c in p[4]])
    fourth = keep([c for p in plans for c in p[6]])

    start(early)
    arrived(far)
    start(relay)
    start(dies[1])
    start(dies[3])
    start(raw)
    arrived(mv_x)
    start(mv_z)
    Z1[:, z] = X1[:, z]
    for p in plans:
        arrived(p[0][:2])
        p[1]()
        start(p[2])

    arrived(relay)
    start(dies[2])

    def slot(s):
        i = inv_ref[0, s]
        return (
            lax.div(i, 32), lax.rem(lax.div(i, 8), 4), lax.rem(lax.div(i, 4), 2), lax.rem(lax.div(i, 2), 2), lax.rem(i, 2),
        )

    def assemble(n, carry):
        j0 = pl.multiple_of(n * 16, 16)
        for h in range(2):
            slots = [slot(2 * (n * 16 + t) + h) for t in range(16)]
            for b0 in range(0, 128, 16):
                got = jnp.swapaxes(jnp.stack([G[i + (pl.ds(b0, 16), slice(None))] for i in slots], axis=0), 0, 1)
                for b in range(16):
                    W[b0 + b, pl.ds(j0, 16), pl.ds(256 * h, 256)] = got[b]
        return carry

    leave = [
        pltpu.make_async_copy(out_v.at[m % 2], out_hbm.at[pl.ds(256 * m, 256), :], out_sem.at[m]) for m in range(4)
    ]

    def project(m):
        tok = (tok_a, tok_b)[m // 2]
        rows = jnp.concatenate([tok[q, pl.ds(256 * (m % 2), 256), :] for q in range(32)], axis=1)
        if m >= 2:
            leave[m - 2].wait()
        out_v[m % 2] = jnp.dot(rows, W[...].reshape(D, KV), preferred_element_type=F32).astype(BF16)
        leave[m].start()

    for d in (0, 1, 3, 2):
        arrived(dies[d])
    inv_copy.wait()
    lax.fori_loop(0, 4, assemble, 0)
    project(0)
    for p in plans:
        arrived(p[0][2:] + p[2])
        p[3]()
        start(p[4])
    project(1)
    project(2)
    for p in plans:
        arrived(p[4])
        p[5]()
        start(p[6])
    project(3)

    arrived(mv_z)
    owner = jnp.dot(
        owner_vec[...].astype(F32).astype(BF16),
        one_hot(iota(sq, 0) == lax.rem(iota(sq, 1), 4) * 32 + iota(sq, 1) // 4),
        preferred_element_type=F32,
    )
    strips = Z1[...].reshape(128, 512)
    halves = [
        jnp.dot(
            one_hot(owner == (2 * iota((64, 128), 0) + h).astype(F32)), strips, preferred_element_type=F32
        ).astype(BF16)
        for h in range(2)
    ]
    for i in range(2):
        for h in range(2):
            m_ref[i, :, pl.ds(256 * h, 256)] = halves[h][:, 256 * i : 256 * i + 256]
    wrow_ref[...] = W[nown_ref[f] * 4 + r]
    for p in plans:
        arrived(p[6])
        p[7]()
    leave[2].wait()
    leave[3].wait()
    for c in everything:
        c.wait_send()


def landing_shapes():
    shapes = []
    at = ("at", 0)
    for (a1, a2, a3), rows, cols in RS_COLORS:
        n, m = rows[1], cols[1]

        def size(spec):
            return tuple(static_sizes(spec))

        half = size({a1: "at", a2: "half", a3: "all"}) + (n, m)
        full = size({a1: "at", a2: "all", a3: "all"}) + (n, m)
        line = size({a1: "at", a2: "at", a3: "all"}) + (n, m)
        shapes += [
            pltpu.VMEM(half, BF16), pltpu.VMEM(half, BF16),
            pltpu.VMEM(full, BF16), pltpu.VMEM(full, BF16),
            pltpu.VMEM((3,) + line, BF16), pltpu.VMEM((3, 1, 1, 1, 1, n, m), BF16),
        ]
    return shapes


def static_sizes(spec):
    sizes = []
    for axis in ("x", "z", "y"):
        kind = spec[axis]
        if axis == "y":
            sizes += {"at": [1, 1], "half": [1, 2], "all": [2, 2]}[kind]
        else:
            sizes += {"at": [1], "half": [2], "all": [4]}[kind]
    return sizes


def fused(new_owner, old_owner, tokens, cotangent, old_weight, old_first, old_second):
    smem = pl.BlockSpec(memory_space=pltpu.SMEM)
    vmem = pl.BlockSpec(memory_space=pltpu.VMEM)
    anywhere = pl.BlockSpec(memory_space=pl.ANY)
    dma = pltpu.SemaphoreType.DMA
    return pl.pallas_call(
        kernel,
        out_shape=(
            jax.ShapeDtypeStruct((ROWS, KV), BF16),
            jax.ShapeDtypeStruct((64, KV), F32),
            jax.ShapeDtypeStruct((2, 64, KV), BF16),
            jax.ShapeDtypeStruct((64, KV), BF16),
        ),
        in_specs=[smem, vmem, vmem] + [anywhere] * 4 + [vmem],
        out_specs=(anywhere, vmem, vmem, vmem),
        scratch_shapes=[
            pltpu.VMEM((ROWS, KV), BF16),
            pltpu.VMEM((64, KV), F32),
            pltpu.VMEM((64, KV), F32),
            pltpu.VMEM((2, 256, KV), BF16),
            dma((3,)),
            dma((4,)),
            pltpu.VMEM((1, 128), jnp.int32),
            pltpu.SMEM((1, 128), jnp.int32),
            dma,
            pltpu.VMEM((32, ROWS // 2, 256), BF16),
            pltpu.VMEM((32, ROWS // 2, 256), BF16),
            pltpu.VMEM((8, 256, KV), F32),
            pltpu.VMEM((4, 4, 2, 2, 2, 128, 256), BF16),
            pltpu.VMEM((128, 64, KV), BF16),
            pltpu.VMEM((4, 4, 2, 2, 2, 64, KV), BF16),
            pltpu.VMEM((4, 4, 2, 2, 64, KV), BF16),
            pltpu.VMEM((4, 4, 2, 2, 64, KV), BF16),
            pltpu.VMEM((2, 2, 2, 16, 512), BF16),
            pltpu.VMEM((2, 2, 2, 16, 512), BF16),
            pltpu.VMEM((2, 2, 2, 16, 512), BF16),
            pltpu.VMEM((4, 4, 8, 512), BF16),
            pltpu.VMEM((4, 4, 8, 512), BF16),
            pltpu.VMEM((4, 4, 8, 512), BF16),
        ]
        + landing_shapes()
        + [
            dma((64,)),
            dma((3, 10)), dma((3, 10)), dma((3, 4)), dma((3, 4)),
            dma((4,)), dma((4,)), dma((3, 12)), dma((3, 12)),
            dma((10,)), dma((10,)),
        ],
        compiler_params=pltpu.CompilerParams(
            collective_id=0, has_side_effects=True, vmem_limit_bytes=67_000_000
        ),
        name="gather_grad_project",
    )(
        new_owner, new_owner.reshape(1, 32), old_owner.reshape(1, 128),
        tokens, cotangent, old_first, old_second, old_weight,
    )


def finish_kernel(
    proj_hbm, grad_hbm, m_hbm, w_hbm, out_hbm, new_w_hbm, new_f_hbm, new_s_hbm,
    proj, grad, m, w, new_w, new_f, new_s, in_sem, out_sem,
):
    tiles = [pl.ds(256 * i, 256) for i in range(4)]
    small = [
        pltpu.make_async_copy(a, b, in_sem.at[i])
        for i, (a, b) in enumerate(((grad_hbm, grad), (m_hbm, m), (w_hbm, w)))
    ]
    enter = [pltpu.make_async_copy(proj_hbm.at[t], proj.at[t], in_sem.at[3 + i]) for i, t in enumerate(tiles)]
    leave = [pltpu.make_async_copy(proj.at[t], out_hbm.at[t], out_sem.at[3 + i]) for i, t in enumerate(tiles)]
    results = [
        pltpu.make_async_copy(a, b, out_sem.at[i])
        for i, (a, b) in enumerate(((new_w, new_w_hbm), (new_f, new_f_hbm), (new_s, new_s_hbm)))
    ]
    for c in small + enter:
        c.start()
    for c in small:
        c.wait()
    gradient = grad[...]
    first_next = beta_one * m[0].astype(F32) + (1.0 - beta_one) * gradient
    second_next = beta_two * m[1].astype(F32) + (1.0 - beta_two) * gradient * gradient
    step_size = first_next / correction_one / (jnp.sqrt(second_next / correction_two) + epsilon)
    new_f[...] = first_next
    new_s[...] = second_next
    new_w[...] = (w[...].astype(F32) * (1.0 - learn_rate * decay_rate) - learn_rate * step_size).astype(BF16)
    for a, b in zip(enter, leave):
        a.wait()
        b.start()
    for c in results:
        c.start()
    for c in results + leave:
        c.wait()


def finish(projected, gradient, moments, weight_rows):
    anywhere = pl.BlockSpec(memory_space=pl.ANY)
    f32, bf16 = pltpu.VMEM((64, KV), F32), pltpu.VMEM((64, KV), BF16)
    return pl.pallas_call(
        finish_kernel,
        out_shape=(
            jax.ShapeDtypeStruct((ROWS, KV), BF16),
            jax.ShapeDtypeStruct((64, KV), BF16),
            jax.ShapeDtypeStruct((64, KV), F32),
            jax.ShapeDtypeStruct((64, KV), F32),
        ),
        in_specs=[anywhere] * 4,
        out_specs=(anywhere,) * 4,
        scratch_shapes=[
            pltpu.VMEM((ROWS, KV), BF16), f32, pltpu.VMEM((2, 64, KV), BF16), bf16, bf16, f32, f32,
            pltpu.SemaphoreType.DMA((7,)), pltpu.SemaphoreType.DMA((7,)),
        ],
        name="adamw",
    )(projected, gradient, moments, weight_rows)


def body(tokens, cotangent, old_weight, old_first, old_second, old_owner, new_owner):
    projected, gradient, moments, weight_rows = fused(
        new_owner, old_owner, tokens, cotangent, old_weight, old_first, old_second
    )
    return finish(projected, gradient, moments, weight_rows)


def solution(mesh):
    rows = P(("rep", "fsdp"), None)
    return jax.shard_map(
        body,
        mesh=mesh,
        in_specs=(rows, rows, rows, rows, rows, P(), P()),
        out_specs=(rows, rows, rows, rows),
        check_vma=False,
    )
```
